32 devices in a mesh: row: 4 (over z), col: 2 (over y), depth: 4 (over x, core).
Axes of the slice: x: 2, y: 2, z: 4, core: 2. Of those that a mesh axis runs over, the one named last changes fastest.
Arguments:
- right_sides: float32 [64, 4096], P('depth', ('row', 'col')), may hold values from -12 to 12
- blocks: float32 [4, 2, 16, 256, 256], P('row', 'col'), may hold values from -0.06 to 6.1, as said below
- block_rows: int32 [4, 2, 16], P('row', 'col'), may hold values from 0 to 3, as said below
- block_cols: int32 [4, 2, 16], P('row', 'col'), may hold values from 0 to 7, as said below
- block_count: int32 [4, 2], P('row', 'col'), may hold values from 2 to 16
Outputs:
- solution: float32 [64, 4096], P('depth', ('row', 'col'))
- residual: float32 [64, 4096], P('depth', ('row', 'col'))
The draws below stay inside these ranges and needn't reach their ends.
Inputs may be any that keep to these rules, and one draw needn't show every extreme that they name: Slot s < 2 of row index r and col index c holds the diagonal block with block_rows = c * 2 + s and block_cols = r * 2 + s. The valid later slots name distinct blocks whose I is below J. At slots from block_count on, block_rows and block_cols hold 0; blocks there hold arbitrary values and are not part of A. `block_cols`: see block_rows. Diagonal-slot blocks are symmetric; A is positive definite. Slots from block_count on are not part of A.
All inputs are finite; a program needn't handle non-finite values.
Results may differ from the reference program's by a relative error of at most 0.0003.
Values sent between devices are 32-bit elements; how exact they have to be, the bound alone decides.
No kernel may reach another device: no remote copies, remote signals or barrier semaphores. Data moves between devices by JAX's collectives and lax.ppermute only.
A program may use at most 64 MiB of HBM per device.

```python
import math
import jax
import jax.numpy as jnp
from jax import lax

NRHS = 64
BLK = 256
ITERS = 2
SEG = 2
SLOTS = 16
NB = 16
NPTS = 4096
N_ROW = 4
N_COL = 2


def block_pattern(key):
    key = jax.random.fold_in(key, 7)
    row_span = SEG * N_COL
    col_span = SEG * N_ROW
    most_extra = SLOTS - SEG
    first_key, second_key, third_key = jax.random.split(key, 3)
    row_tile = jnp.arange(N_ROW, dtype=jnp.int32)[:, None]
    col_tile = jnp.arange(N_COL, dtype=jnp.int32)[None, :]
    avail = (N_ROW - 1 - row_tile) * row_span * SEG + SEG * col_tile * SEG + SEG * (SEG - 1) // 2
    picked = jax.random.randint(first_key, (N_ROW, N_COL), 0, most_extra + 1)
    extra = picked * picked // most_extra
    tile_ids = jnp.arange(N_ROW * N_COL, dtype=jnp.int32).reshape(N_ROW, N_COL)
    tile_score = jax.random.randint(second_key, (N_ROW, N_COL), 0, 1 << 16) * (N_ROW * N_COL) + tile_ids
    tile_score = jnp.where(avail >= most_extra, tile_score, -1 - tile_ids)
    forced = tile_ids == jnp.argmax(tile_score.reshape(-1)).astype(jnp.int32)
    extra = jnp.where(forced, most_extra, jnp.minimum(extra, avail))
    extra = jnp.where(row_tile == 0, jnp.maximum(extra, 1), extra)
    count = (SEG + extra).astype(jnp.int32)
    full_shape = (N_ROW, N_COL, row_span, col_span)
    local_i = jnp.arange(row_span, dtype=jnp.int32)[:, None]
    local_j = jnp.arange(col_span, dtype=jnp.int32)[None, :]
    global_i = jnp.broadcast_to(row_tile[:, :, None, None] * row_span + local_i[None, None], full_shape)
    global_j = jnp.broadcast_to((local_j[None, None] // SEG * N_COL + col_tile[:, :, None, None]) * SEG + local_j[None, None] % SEG, full_shape)
    valid = (global_i < global_j).reshape(N_ROW, N_COL, row_span * col_span)
    far_piece = jnp.broadcast_to((row_tile[:, :, None, None] == 0) & (local_j[None, None] // SEG == N_ROW - 1), full_shape)
    far_piece = far_piece.reshape(N_ROW, N_COL, row_span * col_span)
    flat_ids = jnp.arange(row_span * col_span, dtype=jnp.int32)
    pair_score = jax.random.randint(third_key, (N_ROW, N_COL, row_span * col_span), 0, 1 << 12) * (row_span * col_span) + flat_ids
    pair_score = pair_score + jnp.where(far_piece & valid, 1 << 26, 0).astype(jnp.int32)
    pair_score = jnp.where(valid, pair_score, -1 - flat_ids)
    _, chosen = lax.top_k(pair_score, most_extra)
    keep_slot = jnp.arange(most_extra, dtype=jnp.int32)[None, None, :] < extra[:, :, None]
    other_rows = jnp.where(keep_slot, chosen // col_span, 0).astype(jnp.int32)
    other_cols = jnp.where(keep_slot, chosen % col_span, 0).astype(jnp.int32)
    diag_slot = jnp.arange(SEG, dtype=jnp.int32)[None, None, :]
    diag_rows = jnp.broadcast_to(col_tile[:, :, None] * SEG + diag_slot, (N_ROW, N_COL, SEG))
    diag_cols = jnp.broadcast_to(row_tile[:, :, None] * SEG + diag_slot, (N_ROW, N_COL, SEG))
    rows_all = jnp.concatenate([diag_rows, other_rows], axis=2).astype(jnp.int32)
    cols_all = jnp.concatenate([diag_cols, other_cols], axis=2).astype(jnp.int32)
    return (rows_all, cols_all, count)


def draw_block_rows(key, part):
    return block_pattern(key)[0]


def draw_block_cols(key, part):
    return block_pattern(key)[1]


def draw_block_count(key, part):
    return block_pattern(key)[2]


def draw_blocks(key, part):
    shape = (N_ROW, N_COL, SLOTS, BLK, BLK)
    noise_key, nugget_key = jax.random.split(key, 2)
    noise = jax.random.uniform(noise_key, shape, jnp.float32, -0.014, 0.014)
    nugget = jnp.exp(jax.random.uniform(nugget_key, (N_ROW, N_COL, SLOTS, BLK), jnp.float32, math.log(1.5), math.log(6.0)))
    identity = jnp.eye(BLK, dtype=jnp.float32)
    symmetric = 0.5 * (noise + jnp.swapaxes(noise, -1, -2)) + nugget[..., None] * identity
    diag_slot = (jnp.arange(SLOTS) < SEG)[None, None, :, None, None]
    return jnp.where(diag_slot, symmetric, noise).astype(jnp.float32)


def draw_right_sides(key, part):
    scale_key, value_key = jax.random.split(key, 2)
    scale = jnp.exp(jax.random.uniform(scale_key, (1, NPTS), jnp.float32, math.log(0.3), math.log(3.0)))
    values = jnp.clip(jax.random.normal(value_key, (NRHS, NPTS), jnp.float32), -4.0, 4.0)
    return (values * scale).astype(jnp.float32)


def setup_inputs(seed: int = 0) -> dict:
    splits = jax.random.split(jax.random.key(seed), 6)
    right_sides = draw_right_sides(jax.random.fold_in(splits[5], 71), 0)
    blocks = draw_blocks(jax.random.fold_in(splits[5], 71), 0)
    block_rows = draw_block_rows(jax.random.fold_in(splits[5], 71), 0)
    block_cols = draw_block_cols(jax.random.fold_in(splits[5], 71), 0)
    block_count = draw_block_count(jax.random.fold_in(splits[5], 71), 0)
    return dict(right_sides=right_sides, blocks=blocks, block_rows=block_rows, block_cols=block_cols, block_count=block_count)


def apply_operator(vectors, blocks, block_rows, block_cols, block_count):
    highest = lax.Precision.HIGHEST
    columns = vectors.shape[0]
    row_span = SEG * N_COL
    points = vectors.reshape(columns, NB, BLK)
    slot_index = jnp.arange(SLOTS, dtype=jnp.int32)

    def visit(summed, tile_index):
        row_tile = tile_index // N_COL
        col_tile = tile_index % N_COL
        tile_blocks = blocks[row_tile, col_tile]
        rows_here = block_rows[row_tile, col_tile]
        cols_here = block_cols[row_tile, col_tile]
        live_mask = (slot_index < block_count[row_tile, col_tile]).astype(vectors.dtype)
        mirror_mask = live_mask * (slot_index >= SEG).astype(vectors.dtype)
        global_rows = (row_tile * row_span + rows_here).astype(jnp.int32)
        global_cols = ((cols_here // SEG * N_COL + col_tile) * SEG + cols_here % SEG).astype(jnp.int32)
        toward_rows = jnp.einsum('csk,smk->csm', points[:, global_cols], tile_blocks, precision=highest)
        toward_cols = jnp.einsum('csm,smk->csk', points[:, global_rows], tile_blocks, precision=highest)
        toward_rows = toward_rows * live_mask[None, :, None]
        toward_cols = toward_cols * mirror_mask[None, :, None]
        summed = summed.at[:, global_rows].add(toward_rows).at[:, global_cols].add(toward_cols)
        return (summed, None)
    summed, _ = lax.scan(visit, jnp.zeros_like(points), jnp.arange(N_ROW * N_COL, dtype=jnp.int32))
    return summed.reshape(columns, NPTS)

def reference(right_sides, blocks, block_rows, block_cols, block_count):
    highest = lax.Precision.HIGHEST
    residual = right_sides
    direction = right_sides
    solution = jnp.zeros_like(right_sides)
    current = jnp.dot(residual, residual.T, precision=highest)
    for iteration in range(ITERS):
        mapped = apply_operator(direction, blocks, block_rows, block_cols, block_count)
        curvature = jnp.dot(direction, mapped.T, precision=highest)
        step_size = jax.scipy.linalg.cho_solve((jnp.linalg.cholesky(curvature), True), current)
        solution = solution + jnp.dot(step_size.T, direction, precision=highest)
        residual = residual - jnp.dot(step_size.T, mapped, precision=highest)
        if iteration + 1 < ITERS:
            renewed = jnp.dot(residual, residual.T, precision=highest)
            conjugate = jax.scipy.linalg.cho_solve((jnp.linalg.cholesky(current), True), renewed)
            direction = residual + jnp.dot(conjugate.T, direction, precision=highest)
            current = renewed
    return (solution, residual)
```

```python
import functools

import jax
import jax.numpy as jnp
from jax import lax
from jax.experimental import pallas as pl
from jax.experimental.pallas import tpu as pltpu
from jax.sharding import PartitionSpec as P

BLK = 256
SEG = 2
HIGHEST = lax.Precision.HIGHEST
VMEM = pl.BlockSpec(memory_space=pltpu.VMEM)
SMEM = pl.BlockSpec(memory_space=pltpu.SMEM)
PARAMS = pltpu.CompilerParams(vmem_limit_bytes=40 << 20)


def partner(index, step, size):
    return index ^ step if size & (size - 1) == 0 else (index + step) % size


def source(index, step, size):
    return index ^ step if size & (size - 1) == 0 else (index + size - step) % size


def send_all(arrays, axis):
    size = lax.axis_size(axis)
    return [
        lax.ppermute(arrays[k - 1], axis, [(i, partner(i, k, size)) for i in range(size)])
        for k in range(1, size)
    ]


def source_of(axis, step):
    index, size = lax.axis_index(axis), lax.axis_size(axis)
    if size & (size - 1) == 0:
        return index ^ step
    return lax.rem(index + size - step, size)


def partner_of(axis, step):
    index, size = lax.axis_index(axis), lax.axis_size(axis)
    if size & (size - 1) == 0:
        return index ^ step
    return lax.rem(index + step, size)


def dot_nt(a, b):
    return lax.dot_general(a, b, (((1,), (1,)), ((), ())), precision=HIGHEST, preferred_element_type=jnp.float32)


def dot_tn(a, b):
    return lax.dot_general(a, b, (((0,), (0,)), ((), ())), precision=HIGHEST, preferred_element_type=jnp.float32)


def dot_nn(a, b):
    return lax.dot_general(a, b, (((1,), (0,)), ((), ())), precision=HIGHEST, preferred_element_type=jnp.float32)


def halves(x):
    high = x.astype(jnp.bfloat16)
    return high, (x - high.astype(jnp.float32)).astype(jnp.bfloat16)


def bf16_dot(a, b, contract):
    return lax.dot_general(a, b, (contract, ((), ())), preferred_element_type=jnp.float32)


def stack_fields(all_ref, own_ref, depth_refs):
    width, points = own_ref.shape[0], all_ref.shape[1]
    for step, ref in enumerate([own_ref] + depth_refs):
        place = source_of("depth", step)
        all_ref[pl.ds(pl.multiple_of(place * width, width), width), :] = ref[:, 0:points]


def products(
    n_row, n_col, count_ref, rows_ref, cols_ref, blocks_ref, own_ref, z_refs, y_refs, own_out, z_outs, y_outs,
    col_in, row_in, col_acc, row_acc,
):
    width, points = own_ref.shape[0], SEG * BLK
    row_at, col_at = lax.axis_index("row"), lax.axis_index("col")
    for step, ref in enumerate([own_ref] + z_refs):
        place = source_of("row", step) if step else row_at
        for part in range(SEG):
            high, low = halves(ref[:, part * BLK : (part + 1) * BLK])
            col_in[place * SEG + part] = jnp.concatenate([high, low], axis=0)
    for step, ref in enumerate([own_ref] + y_refs):
        place = source_of("col", step) if step else col_at
        for part in range(SEG):
            high, low = halves(ref[:, part * BLK : (part + 1) * BLK])
            row_in[place * SEG + part] = jnp.concatenate([high, low], axis=0)
    col_acc[...] = jnp.zeros_like(col_acc)
    row_acc[...] = jnp.zeros_like(row_acc)
    count = count_ref[0, 0]
    for slot in range(blocks_ref.shape[0]):
        high, low = halves(blocks_ref[slot])
        row_place, col_place = rows_ref[0, 0, slot], cols_ref[0, 0, slot]
        live = slot < count
        for vec, acc, at_in, at_out, contract in (
            (col_in, row_acc, col_place, row_place, ((1,), (1,))),
            (row_in, col_acc, row_place, col_place, ((1,), (0,))),
        ):
            if slot < SEG and acc is col_acc:
                continue
            both = vec[at_in]
            wide = bf16_dot(both, high, contract)
            term = wide[:width] + wide[width:] + bf16_dot(both[:width], low, contract)
            acc[at_out] += jnp.where(live, term, 0.0)
    for part in range(SEG):
        lanes = slice(part * BLK, (part + 1) * BLK)
        own_out[:, lanes] = row_acc[col_at * SEG + part] + col_acc[row_at * SEG + part]
        for step, ref in enumerate(z_outs, 1):
            ref[:, lanes] = col_acc[partner_of("row", step) * SEG + part]
        for step, ref in enumerate(y_outs, 1):
            ref[:, lanes] = row_acc[partner_of("col", step) * SEG + part]


def split(refs, *sizes):
    out = []
    for size in sizes:
        out.append(list(refs[:size]))
        refs = refs[size:]
    return out


def first_products(n_row, n_col, n_depth, *refs):
    (head, own, z_in, y_in, d_in, outs, z_outs, y_outs, scratch) = split(
        refs, 4, 1, n_row - 1, n_col - 1, n_depth - 1, 2, n_row - 1, n_col - 1, 5
    )
    *scratch, fields = scratch
    points = own[0].shape[1]
    products(n_row, n_col, *head, own[0], z_in, y_in, outs[0], z_outs, y_outs, *scratch)
    stack_fields(fields, own[0], d_in)
    gram = dot_nt(own[0][...], fields[...])
    extra = jnp.concatenate([gram, jnp.zeros_like(gram)], axis=1)
    outs[1][...] = extra
    for ref in z_outs:
        ref[:, points:] = extra


def first_combine(n_row, n_col, n_depth, *refs):
    partial, gram, z_in, y_in, field_refs, out, out_wide, fields = split(
        refs, 1, 1, n_row - 1, n_col - 1, n_depth, 1, 1, 1
    )
    points = partial[0].shape[1]
    total = partial[0][...]
    first = gram[0][:, : gram[0].shape[1] // 2]
    for ref in z_in:
        total += ref[:, :points]
        first += ref[:, points : points + first.shape[1]]
    for ref in y_in:
        total += ref[...]
    stack_fields(fields[0], field_refs[0], field_refs[1:])
    second = dot_nt(total, fields[0][...])
    out[0][...] = total
    out_wide[0][:, :points] = total
    out_wide[0][:, points:] = jnp.concatenate([first, second], axis=1)


def second_products(n_row, n_col, *refs):
    (head, own, z_in, y_in, outs, z_outs, y_outs, scratch) = split(
        refs, 4, 1, n_row - 1, n_col - 1, 2, n_row - 1, n_col - 1, 4
    )
    points = outs[0].shape[1]
    products(n_row, n_col, *head, own[0], z_in, y_in, outs[0], z_outs, y_outs, *scratch)
    grams = own[0][:, points:]
    for ref in y_in:
        grams += ref[:, points:]
    outs[1][...] = grams
    for ref in z_outs:
        ref[:, points:] = grams


def second_combine(n_row, n_col, n_depth, *refs):
    partial, gram, z_in, y_in, base_refs, image_refs, out_wide, out_gram, fields = split(
        refs, 1, 1, n_row - 1, n_col - 1, n_depth, n_depth, 1, 1, 1
    )
    points = partial[0].shape[1]
    half = gram[0].shape[1] // 2
    total = partial[0][...]
    second = gram[0][:, half:]
    for ref in z_in:
        total += ref[:, :points]
        second += ref[:, points + half :]
    for ref in y_in:
        total += ref[...]
    out_wide[0][:, :points] = total
    out_wide[0][:, points:] = jnp.concatenate([gram[0][:, :half], second], axis=1)
    stack_fields(fields[0], base_refs[0], base_refs[1:])
    third = dot_nt(total, fields[0][...])
    stack_fields(fields[0], image_refs[0], image_refs[1:])
    fourth = dot_nt(total, fields[0][...])
    out_gram[0][...] = jnp.concatenate([third, fourth], axis=1)


def eliminate(tables):
    size = tables[0].shape[0]
    at_row = lax.broadcasted_iota(jnp.int32, tables[0].shape, 0)
    for k in range(size):
        for i, table in enumerate(tables):
            pivot_row = table[k : k + 1, :] * (1.0 / table[k : k + 1, k : k + 1])
            tables[i] = jnp.where(at_row == k, pivot_row, table - table[:, k : k + 1] * pivot_row)
    return tables


def finish(n_depth, *refs):
    gathered, wide_refs, base_refs, image_refs, outs, scratch = split(refs, 1, n_depth, n_depth, n_depth, 2, 3)
    base, image, mapped = scratch
    solution_out, residual_out = outs
    width, points = solution_out.shape
    size = n_depth * width
    groups = gathered[0].shape[0] // n_depth
    stack_fields(base, base_refs[0], base_refs[1:])
    stack_fields(image, image_refs[0], image_refs[1:])
    late = [sum(gathered[0][g * n_depth + d] for g in range(groups)) for d in range(n_depth)]
    late = jnp.concatenate(late, axis=0)
    stack_fields(mapped, wide_refs[0], wide_refs[1:])
    early = mapped[:, points:]
    gram0, gram1 = early[:, :size], early[:, size:]
    gram2, gram3 = late[:, :size], late[:, size:]
    gram0, gram1, gram2, gram3 = (0.5 * (g + g.T) for g in (gram0, gram1, gram2, gram3))
    identity = (
        lax.broadcasted_iota(jnp.int32, (size, size), 0) == lax.broadcasted_iota(jnp.int32, (size, size), 1)
    ).astype(jnp.float32)
    first, inverse = eliminate(
        [jnp.concatenate([gram1, gram0], axis=1), jnp.concatenate([gram0, identity], axis=1)]
    )
    step1, inverse = first[:, size:], inverse[:, size:]
    coupling = dot_nn(gram1, step1)
    quadratic = dot_tn(step1, dot_nn(gram2, step1))
    renewed = gram0 - coupling - coupling.T + quadratic
    blend = identity + dot_nn(inverse, renewed)
    upper = dot_nn(gram1, blend) - dot_nn(gram2, step1)
    lower = dot_nn(gram2, blend) - dot_nn(gram3, step1)
    curvature = dot_tn(blend, upper) - dot_tn(step1, lower)
    curvature = 0.5 * (curvature + curvature.T)
    (second,) = eliminate([jnp.concatenate([curvature, renewed], axis=1)])
    own = lax.axis_index("depth") * width
    pick = (
        lax.broadcasted_iota(jnp.int32, (size, width), 0) == lax.broadcasted_iota(jnp.int32, (size, width), 1) + own
    ).astype(jnp.float32)
    step2 = dot_nn(second[:, size:], pick)
    weight0 = dot_nn(step1, pick) + dot_nn(blend, step2)
    weight1 = -dot_nn(step1, step2)
    base_all, image_all = base[...], image[...]
    solution_out[...] = dot_tn(weight0, base_all) + dot_tn(weight1, image_all)
    residual_out[...] = (
        base_refs[0][...] - dot_tn(weight0, image_all) - dot_tn(weight1, mapped[:, :points])
    )


def call(body, name, operands, n_smem, out_shapes, scratch):
    return pl.pallas_call(
        body,
        name=name,
        out_shape=[jax.ShapeDtypeStruct(s, jnp.float32) for s in out_shapes],
        in_specs=[SMEM] * n_smem + [VMEM] * (len(operands) - n_smem),
        out_specs=[VMEM] * len(out_shapes),
        scratch_shapes=scratch,
        compiler_params=PARAMS,
    )(*operands)


def per_device(right_sides, blocks, block_rows, block_cols, block_count):
    n_row, n_col, n_depth = (lax.axis_size(a) for a in ("row", "col", "depth"))
    width, points = right_sides.shape
    size = n_depth * width
    blocks = blocks[0, 0]
    head = [block_count, block_rows, block_cols, blocks]
    f32, b16 = jnp.float32, jnp.bfloat16
    work = [
        pltpu.VMEM((n_row * SEG, 2 * width, BLK), b16),
        pltpu.VMEM((n_col * SEG, 2 * width, BLK), b16),
        pltpu.VMEM((n_row * SEG, width, BLK), f32),
        pltpu.VMEM((n_col * SEG, width, BLK), f32),
    ]
    fields = pltpu.VMEM((size, points), f32)
    narrow, wide, tail = (width, points), (width, points + 2 * size), (width, 2 * size)

    y = send_all([right_sides] * (n_col - 1), "col")
    z = send_all([right_sides] * (n_row - 1), "row")
    base = [right_sides] + send_all([right_sides] * (n_depth - 1), "depth")
    partial, gram, *rest = call(
        functools.partial(first_products, n_row, n_col, n_depth), "first_products",
        head + [right_sides] + z + y + base[1:], 3,
        [narrow, tail] + [wide] * (n_row - 1) + [narrow] * (n_col - 1), work + [fields],
    )
    y = send_all(rest[n_row - 1 :], "col")
    z = send_all(rest[: n_row - 1], "row")
    image, image_wide = call(
        functools.partial(first_combine, n_row, n_col, n_depth), "first_combine",
        [partial, gram] + z + y + base, 0, [narrow, wide], [fields],
    )
    y = send_all([image_wide] * (n_col - 1), "col")
    z = send_all([image] * (n_row - 1), "row")
    image = [image] + send_all([image] * (n_depth - 1), "depth")
    partial, gram, *rest = call(
        functools.partial(second_products, n_row, n_col), "second_products",
        head + [image_wide] + z + y, 3,
        [narrow, tail] + [wide] * (n_row - 1) + [narrow] * (n_col - 1), work,
    )
    y = send_all(rest[n_row - 1 :], "col")
    z = send_all(rest[: n_row - 1], "row")
    mapped, late = call(
        functools.partial(second_combine, n_row, n_col, n_depth), "second_combine",
        [partial, gram] + z + y + base + image, 0, [wide, tail], [fields],
    )
    mapped = [mapped] + send_all([mapped] * (n_depth - 1), "depth")
    everyone = ("row", "col", "depth")
    late = lax.all_to_all(
        jnp.broadcast_to(late[None], (n_row * n_col * n_depth,) + late.shape), everyone, 0, 0
    )
    solution, residual = call(
        functools.partial(finish, n_depth), "finish",
        [late] + mapped + base + image, 0, [narrow, narrow],
        [fields, fields, pltpu.VMEM((size, points + 2 * size), f32)],
    )
    return solution, residual


def solution(mesh):
    return jax.shard_map(
        per_device,
        mesh=mesh,
        in_specs=(
            P("depth", ("row", "col")),
            P("row", "col", None, None, None),
            P("row", "col", None),
            P("row", "col", None),
            P("row", "col"),
        ),
        out_specs=(P("depth", ("row", "col")), P("depth", ("row", "col"))),
        check_vma=False,
    )
```

```python
import functools

import jax
import jax.numpy as jnp
from jax import lax
from jax.experimental import pallas as pl
from jax.experimental.pallas import tpu as pltpu
from jax.sharding import PartitionSpec as P

BLK = 256
SEG = 2
HIGHEST = lax.Precision.HIGHEST
VMEM = pl.BlockSpec(memory_space=pltpu.VMEM)
SMEM = pl.BlockSpec(memory_space=pltpu.SMEM)
PARAMS = pltpu.CompilerParams(vmem_limit_bytes=40 << 20)


def partner(index, step, size):
    return index ^ step if size & (size - 1) == 0 else (index + step) % size


def source(index, step, size):
    return index ^ step if size & (size - 1) == 0 else (index + size - step) % size


def send_all(arrays, axis):
    size = lax.axis_size(axis)
    return [
        lax.ppermute(arrays[k - 1], axis, [(i, partner(i, k, size)) for i in range(size)])
        for k in range(1, size)
    ]


def source_of(axis, step):
    index, size = lax.axis_index(axis), lax.axis_size(axis)
    if size & (size - 1) == 0:
        return index ^ step
    return lax.rem(index + size - step, size)


def partner_of(axis, step):
    index, size = lax.axis_index(axis), lax.axis_size(axis)
    if size & (size - 1) == 0:
        return index ^ step
    return lax.rem(index + step, size)


def dot_nt(a, b):
    return lax.dot_general(a, b, (((1,), (1,)), ((), ())), precision=HIGHEST, preferred_element_type=jnp.float32)


def dot_tn(a, b):
    return lax.dot_general(a, b, (((0,), (0,)), ((), ())), precision=HIGHEST, preferred_element_type=jnp.float32)


def dot_nn(a, b):
    return lax.dot_general(a, b, (((1,), (0,)), ((), ())), precision=HIGHEST, preferred_element_type=jnp.float32)


def halves(x):
    high = x.astype(jnp.bfloat16)
    return high, (x - high.astype(jnp.float32)).astype(jnp.bfloat16)


def bf16_dot(a, b, contract):
    return lax.dot_general(a, b, (contract, ((), ())), preferred_element_type=jnp.float32)


def stack_fields(all_ref, own_ref, depth_refs):
    width, points = own_ref.shape[0], all_ref.shape[1]
    for step, ref in enumerate([own_ref] + depth_refs):
        place = source_of("depth", step)
        all_ref[pl.ds(pl.multiple_of(place * width, width), width), :] = ref[:, 0:points]


def prepare(
    count_ref, rows_ref, cols_ref, blocks_ref, fields_ref, high_out, low_out, fields_out, table_out,
    landed, rows_at, cols_at, sems,
):
    slots = blocks_ref.shape[2]
    copies = [pltpu.make_async_copy(blocks_ref.at[0, 0, s], landed.at[s], sems.at[s]) for s in range(slots)]
    copies.append(pltpu.make_async_copy(rows_ref, rows_at, sems.at[slots]))
    copies.append(pltpu.make_async_copy(cols_ref, cols_at, sems.at[slots + 1]))
    copies.append(pltpu.make_async_copy(fields_ref, fields_out, sems.at[slots + 2]))
    for copy in copies:
        copy.start()
    for slot in range(slots):
        copies[slot].wait()
        high_out[slot], low_out[slot] = halves(landed[slot])
    for copy in copies[slots:]:
        copy.wait()
    for slot in range(slots):
        table_out[0, slot] = rows_at[0, 0, slot]
        table_out[1, slot] = cols_at[0, 0, slot]
        table_out[2, slot] = count_ref[0, 0]


def products(
    n_row, n_col, table_ref, high_ref, low_ref, own_ref, z_refs, y_refs, own_out, z_outs, y_outs,
    col_in, row_in, col_acc, row_acc,
):
    width = own_ref.shape[0]
    row_at, col_at = lax.axis_index("row"), lax.axis_index("col")
    for axis, refs, held in (("row", [own_ref] + z_refs, col_in), ("col", [own_ref] + y_refs, row_in)):
        for step, ref in enumerate(refs):
            place = source_of(axis, step)
            for part in range(SEG):
                high, low = halves(ref[:, part * BLK : (part + 1) * BLK])
                held[place * SEG + part] = jnp.concatenate([high, low], axis=0)
    col_acc[...] = jnp.zeros_like(col_acc)
    row_acc[...] = jnp.zeros_like(row_acc)
    count = table_ref[2, 0]
    for slot in range(high_ref.shape[0]):
        high, low = high_ref[slot], low_ref[slot]
        row_place, col_place = table_ref[0, slot], table_ref[1, slot]
        live = slot < count
        for vec, acc, at_in, at_out, contract in (
            (col_in, row_acc, col_place, row_place, ((1,), (1,))),
            (row_in, col_acc, row_place, col_place, ((1,), (0,))),
        ):
            if slot < SEG and acc is col_acc:
                continue
            both = vec[at_in]
            wide = bf16_dot(both, high, contract)
            term = wide[:width] + wide[width:] + bf16_dot(both[:width], low, contract)
            acc[at_out] += jnp.where(live, term, 0.0)
    for part in range(SEG):
        lanes = slice(part * BLK, (part + 1) * BLK)
        own_out[:, lanes] = row_acc[col_at * SEG + part] + col_acc[row_at * SEG + part]
        for step, ref in enumerate(z_outs, 1):
            ref[:, lanes] = col_acc[partner_of("row", step) * SEG + part]
        for step, ref in enumerate(y_outs, 1):
            ref[:, lanes] = row_acc[partner_of("col", step) * SEG + part]


def split(refs, *sizes):
    out = []
    for size in sizes:
        out.append(list(refs[:size]))
        refs = refs[size:]
    return out


def first_products(n_row, n_col, *refs):
    (head, own, z_in, y_in, outs, z_outs, y_outs, scratch) = split(
        refs, 3, 1, n_row - 1, n_col - 1, 1, n_row - 1, n_col - 1, 4
    )
    products(n_row, n_col, *head, own[0], z_in, y_in, outs[0], z_outs, y_outs, *scratch)


def first_combine(n_row, n_col, n_depth, *refs):
    partial, z_in, y_in, field_refs, out, out_wide, fields = split(refs, 1, n_row - 1, n_col - 1, n_depth, 1, 1, 1)
    points = partial[0].shape[1]
    total = partial[0][...]
    for ref in z_in + y_in:
        total += ref[...]
    stack_fields(fields[0], field_refs[0], field_refs[1:])
    everything = fields[0][...]
    out[0][...] = total
    out_wide[0][:, :points] = total
    out_wide[0][:, points:] = jnp.concatenate(
        [dot_nt(field_refs[0][...], everything), dot_nt(total, everything)], axis=1
    )


def second_products(n_row, n_col, *refs):
    (head, own, z_in, y_in, outs, z_outs, y_outs, scratch) = split(
        refs, 3, 1, n_row - 1, n_col - 1, 2, n_row - 1, n_col - 1, 4
    )
    points = outs[0].shape[1]
    products(n_row, n_col, *head, own[0], z_in, y_in, outs[0], z_outs, y_outs, *scratch)
    grams = own[0][:, points:]
    for ref in y_in:
        grams += ref[:, points:]
    outs[1][...] = grams
    for ref in z_outs:
        ref[:, points:] = grams


def second_combine(n_row, n_col, n_depth, *refs):
    partial, gram, z_in, y_in, base_refs, image_refs, out_wide, out_gram, fields = split(
        refs, 1, 1, n_row - 1, n_col - 1, n_depth, n_depth, 1, 1, 1
    )
    points = partial[0].shape[1]
    total = partial[0][...]
    early = gram[0][...]
    for ref in z_in:
        total += ref[:, :points]
        early += ref[:, points:]
    for ref in y_in:
        total += ref[...]
    out_wide[0][:, :points] = total
    out_wide[0][:, points:] = early
    stack_fields(fields[0], base_refs[0], base_refs[1:])
    third = dot_nt(total, fields[0][...])
    stack_fields(fields[0], image_refs[0], image_refs[1:])
    fourth = dot_nt(total, fields[0][...])
    late = jnp.concatenate([third, fourth], axis=1)
    for i in range(out_gram[0].shape[0]):
        out_gram[0][i] = late


def eliminate(tables):
    size, wide = tables[0].shape
    sub = 8
    at_row = lax.broadcasted_iota(jnp.int32, (sub, wide), 0)
    tables = [[table[t : t + sub] for t in range(0, size, sub)] for table in tables]
    for k in range(0, size, 4):
        home, base = k // sub, k % sub
        for tiles in tables:
            spread = [[jnp.broadcast_to(tile[:, k + j : k + j + 1], (sub, wide)) for tile in tiles] for j in range(4)]
            row = [jnp.broadcast_to(tiles[home][base + i : base + i + 1], (sub, wide)) for i in range(4)]
            e = [
                [jnp.broadcast_to(spread[j][home][base + i : base + i + 1], (sub, wide)) if i <= j else None for j in range(4)]
                for i in range(4)
            ]
            scale = 1.0 / (e[0][0] * e[1][1] - e[0][1] * e[0][1])
            a00, a01, a11 = e[1][1] * scale, -e[0][1] * scale, e[0][0] * scale
            x00, x10 = a00 * e[0][2] + a01 * e[1][2], a01 * e[0][2] + a11 * e[1][2]
            x01, x11 = a00 * e[0][3] + a01 * e[1][3], a01 * e[0][3] + a11 * e[1][3]
            s00 = e[2][2] - (e[0][2] * x00 + e[1][2] * x10)
            s01 = e[2][3] - (e[0][2] * x01 + e[1][2] * x11)
            s11 = e[3][3] - (e[0][3] * x01 + e[1][3] * x11)
            scale = 1.0 / (s00 * s11 - s01 * s01)
            t2 = row[2] - (x00 * row[0] + x10 * row[1])
            t3 = row[3] - (x01 * row[0] + x11 * row[1])
            p2 = (s11 * t2 - s01 * t3) * scale
            p3 = (s00 * t3 - s01 * t2) * scale
            p0 = (a00 * row[0] + a01 * row[1]) - (x00 * p2 + x01 * p3)
            p1 = (a01 * row[0] + a11 * row[1]) - (x10 * p2 + x11 * p3)
            pivots = (p0, p1, p2, p3)
            for t, tile in enumerate(tiles):
                if t == home:
                    keep = tile - sum(spread[j][t] * pivots[j] for j in range(4))
                    for i in range(4):
                        keep = jnp.where(at_row == base + i, pivots[i], keep)
                    tiles[t] = keep
                else:
                    tiles[t] = tile - sum(spread[j][t] * pivots[j] for j in range(4))
    return [jnp.concatenate(tiles, axis=0) for tiles in tables]


def identity_of(size):
    shape = (size, size)
    same = lax.broadcasted_iota(jnp.int32, shape, 0) == lax.broadcasted_iota(jnp.int32, shape, 1)
    return same.astype(jnp.float32)


def early_solve(n_depth, points, *refs):
    wide_refs, outs, scratch = split(refs, n_depth, 4, 1)
    width = wide_refs[0].shape[0]
    for step, ref in enumerate(wide_refs):
        place = source_of("depth", step)
        scratch[0][pl.ds(pl.multiple_of(place * width, width), width), :] = ref[:, points:]
    early = scratch[0][...]
    size = n_depth * width
    gram0, gram1 = early[:, :size], early[:, size:]
    first, inverse = eliminate(
        [jnp.concatenate([gram1, gram0], axis=1), jnp.concatenate([gram0, identity_of(size)], axis=1)]
    )
    step1 = first[:, size:]
    coupling = dot_nn(gram1, step1)
    outs[0][...] = step1
    outs[1][...] = inverse[:, size:]
    outs[2][...] = gram0 - coupling - coupling.T
    outs[3][...] = gram1


def finish(n_depth, *refs):
    gathered, solved, wide_refs, base_refs, image_refs, outs, scratch = split(
        refs, 1, 4, n_depth, n_depth, n_depth, 2, 3
    )
    base, image, mapped = scratch
    solution_out, residual_out = outs
    width, points = solution_out.shape
    size = n_depth * width
    groups = gathered[0].shape[0] // n_depth
    stack_fields(base, base_refs[0], base_refs[1:])
    stack_fields(image, image_refs[0], image_refs[1:])
    stack_fields(mapped, wide_refs[0], wide_refs[1:])
    late = [sum(gathered[0][g * n_depth + d] for g in range(groups)) for d in range(n_depth)]
    late = jnp.concatenate(late, axis=0)
    gram2, gram3 = late[:, :size], late[:, size:]
    step1, inverse, rest, gram1 = (ref[...] for ref in solved)
    product = dot_nn(gram2, step1)
    renewed = rest + dot_tn(step1, product)
    blend = identity_of(size) + dot_nn(inverse, renewed)
    upper = dot_nn(gram1, blend) - product
    lower = dot_nn(gram2, blend) - dot_nn(gram3, step1)
    curvature = dot_tn(blend, upper) - dot_tn(step1, lower)
    (second,) = eliminate([jnp.concatenate([curvature, renewed], axis=1)])
    own = lax.axis_index("depth") * width
    pick = (
        lax.broadcasted_iota(jnp.int32, (size, width), 0) == lax.broadcasted_iota(jnp.int32, (size, width), 1) + own
    ).astype(jnp.float32)
    step2 = dot_nn(second[:, size:], pick)
    weight0 = dot_nn(step1, pick) + dot_nn(blend, step2)
    weight1 = -dot_nn(step1, step2)
    base_all, image_all = base[...], image[...]
    solution_out[...] = dot_tn(weight0, base_all) + dot_tn(weight1, image_all)
    residual_out[...] = base_refs[0][...] - dot_tn(weight0, image_all) - dot_tn(weight1, mapped[...])


def call(body, name, operands, in_specs, out_shapes, scratch, cost=None, out_specs=None):
    return pl.pallas_call(
        body,
        name=name,
        out_shape=[s if hasattr(s, "dtype") else jax.ShapeDtypeStruct(s, jnp.float32) for s in out_shapes],
        in_specs=list(in_specs) + [VMEM] * (len(operands) - len(in_specs)),
        out_specs=out_specs or [VMEM] * len(out_shapes),
        scratch_shapes=scratch,
        compiler_params=PARAMS,
        cost_estimate=cost,
    )(*operands)


def per_device(right_sides, blocks, block_rows, block_cols, block_count):
    n_row, n_col, n_depth = (lax.axis_size(a) for a in ("row", "col", "depth"))
    width, points = right_sides.shape
    size = n_depth * width
    slots = blocks.shape[2]
    f32, b16 = jnp.float32, jnp.bfloat16
    work = [
        pltpu.VMEM((n_row * SEG, 2 * width, BLK), b16),
        pltpu.VMEM((n_col * SEG, 2 * width, BLK), b16),
        pltpu.VMEM((n_row * SEG, width, BLK), f32),
        pltpu.VMEM((n_col * SEG, width, BLK), f32),
    ]
    fields = pltpu.VMEM((size, points), f32)
    narrow, wide, tail, square = (width, points), (width, points + 2 * size), (width, 2 * size), (size, size)

    y = send_all([right_sides] * (n_col - 1), "col")
    z = send_all([right_sides] * (n_row - 1), "row")
    half = jax.ShapeDtypeStruct(blocks.shape[2:], b16)
    high, low, fields_copy, table = call(
        prepare, "prepare",
        [block_count]
        + [pltpu.with_memory_space_constraint(x, pltpu.HBM) for x in (block_rows, block_cols, blocks, right_sides)],
        [SMEM] + [pl.BlockSpec(memory_space=pltpu.HBM)] * 4,
        [half, half, narrow, jax.ShapeDtypeStruct((3, slots), jnp.int32)],
        [pltpu.VMEM(blocks.shape[2:], f32)]
        + [pltpu.SMEM(block_rows.shape, jnp.int32)] * 2 + [pltpu.SemaphoreType.DMA((slots + 3,))],
        pl.CostEstimate(flops=4 * blocks.size, transcendentals=0, bytes_accessed=8 * blocks.size),
        [VMEM] * 3 + [SMEM],
    )
    head = [table, high, low]
    base = [right_sides] + send_all([fields_copy] * (n_depth - 1), "depth")
    partial, *rest = call(
        functools.partial(first_products, n_row, n_col), "first_products",
        head + [right_sides] + z + y, [SMEM], [narrow] * (n_row + n_col - 1), work,
    )
    y = send_all(rest[n_row - 1 :], "col")
    z = send_all(rest[: n_row - 1], "row")
    image, image_wide = call(
        functools.partial(first_combine, n_row, n_col, n_depth), "first_combine",
        [partial] + z + y + base, [], [narrow, wide], [fields],
    )
    y = send_all([image_wide] * (n_col - 1), "col")
    z = send_all([image] * (n_row - 1), "row")
    image = [image] + send_all([image] * (n_depth - 1), "depth")
    partial, gram, *rest = call(
        functools.partial(second_products, n_row, n_col), "second_products",
        head + [image_wide] + z + y, [SMEM],
        [narrow, tail] + [wide] * (n_row - 1) + [narrow] * (n_col - 1), work,
    )
    y = send_all(rest[n_row - 1 :], "col")
    z = send_all(rest[: n_row - 1], "row")
    n_all = n_row * n_col * n_depth
    mapped, late = call(
        functools.partial(second_combine, n_row, n_col, n_depth), "second_combine",
        [partial, gram] + z + y + base + image, [], [wide, (n_all,) + tail], [fields],
    )
    mapped = [mapped] + send_all([mapped] * (n_depth - 1), "depth")
    late = lax.all_to_all(late, ("row", "col", "depth"), 0, 0)
    solved = call(
        functools.partial(early_solve, n_depth, points), "early_solve", mapped, [], [square] * 4,
        [pltpu.VMEM((size, 2 * size), f32)],
        pl.CostEstimate(flops=4 * size**3, transcendentals=0, bytes_accessed=160 * size * size),
    )
    solution, residual = call(
        functools.partial(finish, n_depth), "finish",
        [late] + list(solved) + mapped + base + image, [], [narrow, narrow], [fields, fields, fields],
    )
    return solution, residual


def solution(mesh):
    return jax.shard_map(
        per_device,
        mesh=mesh,
        in_specs=(
            P("depth", ("row", "col")),
            P("row", "col", None, None, None),
            P("row", "col", None),
            P("row", "col", None),
            P("row", "col"),
        ),
        out_specs=(P("depth", ("row", "col")), P("depth", ("row", "col"))),
        check_vma=False,
    )
```

```python
import functools

import jax
import jax.numpy as jnp
from jax import lax
from jax.experimental import pallas as pl
from jax.experimental.pallas import tpu as pltpu
from jax.sharding import PartitionSpec as P


BLK = 256
SEG = 2
HIGHEST = lax.Precision.HIGHEST
VMEM = pl.BlockSpec(memory_space=pltpu.VMEM)
SMEM = pl.BlockSpec(memory_space=pltpu.SMEM)
PARAMS = pltpu.CompilerParams(vmem_limit_bytes=40 << 20)


def partner(index, step, size):
    return index ^ step if size & (size - 1) == 0 else (index + step) % size


def power_of_two(n):
    return n & (n - 1) == 0


def send_all(arrays, axis):
    size = lax.axis_size(axis)
    return [send(arrays[k - 1], axis, k) for k in range(1, size)]


def send(x, axis, step):
    size = lax.axis_size(axis)
    return lax.ppermute(x, axis, [(i, partner(i, step, size)) for i in range(size)])


def collect(x, axis):
    size = lax.axis_size(axis)
    if not power_of_two(size):
        return send_all([x] * (size - 1), axis)
    held = {0: x}
    for k in sorted(range(1, size), key=lambda k: (k.bit_count(), -k)):
        low = k & -k
        held[k] = send(held[k - low], axis, low)
    return [held[k] for k in range(1, size)]


def source_of(axis, step):
    index, size = lax.axis_index(axis), lax.axis_size(axis)
    if size & (size - 1) == 0:
        return index ^ step
    return lax.rem(index + size - step, size)


def partner_of(axis, step):
    index, size = lax.axis_index(axis), lax.axis_size(axis)
    if size & (size - 1) == 0:
        return index ^ step
    return lax.rem(index + step, size)


def dot_nt(a, b):
    return lax.dot_general(a, b, (((1,), (1,)), ((), ())), precision=HIGHEST, preferred_element_type=jnp.float32)


def dot_tn(a, b):
    return lax.dot_general(a, b, (((0,), (0,)), ((), ())), precision=HIGHEST, preferred_element_type=jnp.float32)


def dot_nn(a, b):
    return lax.dot_general(a, b, (((1,), (0,)), ((), ())), precision=HIGHEST, preferred_element_type=jnp.float32)


def halves(x):
    high = x.astype(jnp.bfloat16)
    return high, (x - high.astype(jnp.float32)).astype(jnp.bfloat16)


def bf16_dot(a, b, contract):
    return lax.dot_general(a, b, (contract, ((), ())), preferred_element_type=jnp.float32)


def stack_fields(all_ref, own_ref, depth_refs):
    width, points = own_ref.shape[0], all_ref.shape[1]
    for step, ref in enumerate([own_ref] + depth_refs):
        place = source_of("depth", step)
        all_ref[pl.ds(pl.multiple_of(place * width, width), width), :] = ref[:, 0:points]


def prepare(count_ref, rows_ref, cols_ref, blocks_ref, blocks_out, table_out, rows_at, cols_at, sems):
    slots = blocks_ref.shape[2]
    copies = [pltpu.make_async_copy(blocks_ref.at[0, 0, s], blocks_out.at[s], sems.at[s]) for s in range(slots)]
    small = [
        pltpu.make_async_copy(rows_ref, rows_at, sems.at[slots]),
        pltpu.make_async_copy(cols_ref, cols_at, sems.at[slots + 1]),
    ]
    for copy in small + copies:
        copy.start()
    for copy in small:
        copy.wait()
    for slot in range(slots):
        table_out[0, slot] = rows_at[0, 0, slot]
        table_out[1, slot] = cols_at[0, 0, slot]
        table_out[2, slot] = count_ref[0, 0]
    for copy in copies:
        copy.wait()


def products(
    table_ref, blocks_ref, own_ref, z_refs, y_refs, own_out, z_outs, y_outs,
    col_in, row_in, col_acc, row_acc,
):
    width = own_ref.shape[0]
    row_at, col_at = lax.axis_index("row"), lax.axis_index("col")
    for axis, refs, held in (("row", [own_ref] + z_refs, col_in), ("col", [own_ref] + y_refs, row_in)):
        for step, ref in enumerate(refs):
            place = source_of(axis, step)
            for part in range(SEG):
                high, low = halves(ref[:, part * BLK : (part + 1) * BLK])
                held[place * SEG + part] = jnp.concatenate([high, low], axis=0)
    col_acc[...] = jnp.zeros_like(col_acc)
    row_acc[...] = jnp.zeros_like(row_acc)
    count = table_ref[2, 0]
    for slot in range(blocks_ref.shape[0]):
        high, low = halves(blocks_ref[slot])
        row_place, col_place = table_ref[0, slot], table_ref[1, slot]
        live = slot < count
        for vec, acc, at_in, at_out, contract in (
            (col_in, row_acc, col_place, row_place, ((1,), (1,))),
            (row_in, col_acc, row_place, col_place, ((1,), (0,))),
        ):
            if slot < SEG and acc is col_acc:
                continue
            both = vec[at_in]
            wide = bf16_dot(both, high, contract)
            term = wide[:width] + wide[width:] + bf16_dot(both[:width], low, contract)
            acc[at_out] += jnp.where(live, term, 0.0)
    for part in range(SEG):
        lanes = slice(part * BLK, (part + 1) * BLK)
        own_out[:, lanes] = row_acc[col_at * SEG + part] + col_acc[row_at * SEG + part]
        for step, ref in enumerate(z_outs, 1):
            ref[:, lanes] = col_acc[partner_of("row", step) * SEG + part]
        for step, ref in enumerate(y_outs, 1):
            ref[:, lanes] = row_acc[partner_of("col", step) * SEG + part]


def split(refs, *sizes):
    out = []
    for size in sizes:
        out.append(list(refs[:size]))
        refs = refs[size:]
    return out


def first_products(n_row, n_col, *refs):
    (head, own, z_in, y_in, outs, z_outs, y_outs, scratch) = split(
        refs, 2, 1, n_row - 1, n_col - 1, 2, n_row - 1, n_col - 1, 4
    )
    outs[1][...] = own[0][...]
    products(*head, own[0], z_in, y_in, outs[0], z_outs, y_outs, *scratch)


def first_combine(n_row, n_col, *refs):
    partial, received, out = split(refs, 1, n_row + n_col - 2, 1)
    total = partial[0][...]
    for ref in received:
        total += ref[...]
    out[0][...] = total


def first_grams(n_depth, *refs):
    image, field_refs, out, fields = split(refs, 1, n_depth, 1, 1)
    total = image[0][...]
    points = total.shape[1]
    stack_fields(fields[0], field_refs[0], field_refs[1:])
    everything = fields[0][...]
    out[0][:, :points] = total
    out[0][:, points:] = jnp.concatenate(
        [dot_nt(field_refs[0][...], everything), dot_nt(total, everything)], axis=1
    )


def second_products(n_row, n_col, *refs):
    (head, own, z_in, y_in, outs, z_outs, y_outs, scratch) = split(
        refs, 2, 1, n_row - 1, n_col - 1, 2, n_row - 1, n_col - 1, 4
    )
    points = outs[0].shape[1]
    products(*head, own[0], z_in, y_in, outs[0], z_outs, y_outs, *scratch)
    grams = own[0][:, points:]
    for ref in y_in:
        grams += ref[:, points:]
    outs[1][...] = grams
    for ref in z_outs:
        ref[:, points:] = grams


def second_combine(n_row, n_col, n_depth, *refs):
    partial, gram, z_in, y_in, base_refs, image_refs, out_wide, out_gram, fields = split(
        refs, 1, 1, n_row - 1, n_col - 1, n_depth, n_depth, 1, 1, 1
    )
    points = partial[0].shape[1]
    total = partial[0][...]
    early = gram[0][...]
    for ref in z_in:
        total += ref[:, :points]
        early += ref[:, points:]
    for ref in y_in:
        total += ref[...]
    out_wide[0][:, :points] = total
    out_wide[0][:, points:] = early
    stack_fields(fields[0], base_refs[0], base_refs[1:])
    third = dot_nt(total, fields[0][...])
    stack_fields(fields[0], image_refs[0], image_refs[1:])
    fourth = dot_nt(total, fields[0][...])
    late = jnp.concatenate([third, fourth], axis=1)
    for i in range(out_gram[0].shape[0]):
        out_gram[0][i] = late


def eliminate(tables):
    size, wide = tables[0].shape
    sub = 8
    at_row = lax.broadcasted_iota(jnp.int32, (sub, wide), 0)
    tables = [[table[t : t + sub] for t in range(0, size, sub)] for table in tables]
    for k in range(0, size, 4):
        home, base = k // sub, k % sub
        for tiles in tables:
            spread = [[jnp.broadcast_to(tile[:, k + j : k + j + 1], (sub, wide)) for tile in tiles] for j in range(4)]
            row = [jnp.broadcast_to(tiles[home][base + i : base + i + 1], (sub, wide)) for i in range(4)]
            e = [
                [jnp.broadcast_to(spread[j][home][base + i : base + i + 1], (sub, wide)) if i <= j else None for j in range(4)]
                for i in range(4)
            ]
            scale = 1.0 / (e[0][0] * e[1][1] - e[0][1] * e[0][1])
            a00, a01, a11 = e[1][1] * scale, -e[0][1] * scale, e[0][0] * scale
            x00, x10 = a00 * e[0][2] + a01 * e[1][2], a01 * e[0][2] + a11 * e[1][2]
            x01, x11 = a00 * e[0][3] + a01 * e[1][3], a01 * e[0][3] + a11 * e[1][3]
            s00 = e[2][2] - (e[0][2] * x00 + e[1][2] * x10)
            s01 = e[2][3] - (e[0][2] * x01 + e[1][2] * x11)
            s11 = e[3][3] - (e[0][3] * x01 + e[1][3] * x11)
            scale = 1.0 / (s00 * s11 - s01 * s01)
            t2 = row[2] - (x00 * row[0] + x10 * row[1])
            t3 = row[3] - (x01 * row[0] + x11 * row[1])
            p2 = (s11 * t2 - s01 * t3) * scale
            p3 = (s00 * t3 - s01 * t2) * scale
            p0 = (a00 * row[0] + a01 * row[1]) - (x00 * p2 + x01 * p3)
            p1 = (a01 * row[0] + a11 * row[1]) - (x10 * p2 + x11 * p3)
            pivots = (p0, p1, p2, p3)
            for t, tile in enumerate(tiles):
                if t == home:
                    keep = tile - sum(spread[j][t] * pivots[j] for j in range(4))
                    for i in range(4):
                        keep = jnp.where(at_row == base + i, pivots[i], keep)
                    tiles[t] = keep
                else:
                    tiles[t] = tile - sum(spread[j][t] * pivots[j] for j in range(4))
    return [jnp.concatenate(tiles, axis=0) for tiles in tables]


def identity_of(size):
    shape = (size, size)
    same = lax.broadcasted_iota(jnp.int32, shape, 0) == lax.broadcasted_iota(jnp.int32, shape, 1)
    return same.astype(jnp.float32)


def early_solve(n_depth, points, *refs):
    wide_refs, outs, scratch = split(refs, n_depth, 3, 1)
    width = wide_refs[0].shape[0]
    size = n_depth * width
    for step, ref in enumerate(wide_refs):
        place = source_of("depth", step)
        scratch[0][pl.ds(pl.multiple_of(place * width, width), width), :] = ref[:, points + size : points + 2 * size]
    gram1 = scratch[0][...]
    (first,) = eliminate([jnp.concatenate([gram1, identity_of(size)], axis=1)])
    inverse = first[:, size:]
    outs[0][...] = inverse
    outs[1][...] = dot_nt(inverse, wide_refs[0][:, points : points + size])
    outs[2][...] = dot_nt(identity_of(size), wide_refs[0][:, points + size : points + 2 * size])


def finish(n_depth, *refs):
    gathered, solved, wide_refs, base_refs, image_refs, outs, scratch = split(
        refs, 1, 3, n_depth, n_depth, n_depth, 2, 3
    )
    base, image, mapped = scratch
    solution_out, residual_out = outs
    width, _ = solution_out.shape
    size = n_depth * width
    groups = gathered[0].shape[0] // n_depth
    stack_fields(base, base_refs[0], base_refs[1:])
    stack_fields(image, image_refs[0], image_refs[1:])
    stack_fields(mapped, wide_refs[0], wide_refs[1:])
    late = [sum(gathered[0][g * n_depth + d] for g in range(groups)) for d in range(n_depth)]
    late = jnp.concatenate(late, axis=0)
    gram2, gram3 = late[:, :size], late[:, size:]
    inverse, start, gram1_own = (ref[...] for ref in solved)
    carry = dot_nn(inverse, gram2)
    schur = gram3 - dot_nn(gram2, carry)
    right = gram1_own - dot_nn(gram2, start)
    fill = jnp.zeros((size, size - width), jnp.float32)
    (second,) = eliminate([jnp.concatenate([schur, right, fill], axis=1)])
    weight1 = second[:, size : size + width]
    weight0 = start - dot_nn(carry, weight1)
    base_all, image_all = base[...], image[...]
    solution_out[...] = dot_tn(weight0, base_all) + dot_tn(weight1, image_all)
    residual_out[...] = base_refs[0][...] - dot_tn(weight0, image_all) - dot_tn(weight1, mapped[...])


def call(body, operands, in_specs, out_shapes, scratch, cost=None, out_specs=None):
    return pl.pallas_call(
        body,
        out_shape=[s if hasattr(s, "dtype") else jax.ShapeDtypeStruct(s, jnp.float32) for s in out_shapes],
        in_specs=list(in_specs) + [VMEM] * (len(operands) - len(in_specs)),
        out_specs=out_specs or [VMEM] * len(out_shapes),
        scratch_shapes=scratch,
        compiler_params=PARAMS,
        cost_estimate=cost,
    )(*operands)


def per_device(right_sides, blocks, block_rows, block_cols, block_count):
    n_row, n_col, n_depth = (lax.axis_size(a) for a in ("row", "col", "depth"))
    width, points = right_sides.shape
    size = n_depth * width
    slots = blocks.shape[2]
    f32, b16 = jnp.float32, jnp.bfloat16
    work = [
        pltpu.VMEM((n_row * SEG, 2 * width, BLK), b16),
        pltpu.VMEM((n_col * SEG, 2 * width, BLK), b16),
        pltpu.VMEM((n_row * SEG, width, BLK), f32),
        pltpu.VMEM((n_col * SEG, width, BLK), f32),
    ]
    fields = pltpu.VMEM((size, points), f32)
    narrow, wide, tail, square = (width, points), (width, points + 2 * size), (width, 2 * size), (size, size)

    y = send_all([right_sides] * (n_col - 1), "col")
    z = send_all([right_sides] * (n_row - 1), "row")
    near, table = call(
        prepare,
        [block_count] + [pltpu.with_memory_space_constraint(x, pltpu.HBM) for x in (block_rows, block_cols, blocks)],
        [SMEM] + [pl.BlockSpec(memory_space=pltpu.HBM)] * 3,
        [blocks.shape[2:], jax.ShapeDtypeStruct((3, slots), jnp.int32)],
        [pltpu.SMEM(block_rows.shape, jnp.int32)] * 2 + [pltpu.SemaphoreType.DMA((slots + 2,))],
        pl.CostEstimate(flops=0, transcendentals=0, bytes_accessed=8 * blocks.size),
        [VMEM, SMEM],
    )
    head = [table, near]
    partial, copied, *rest = call(
        functools.partial(first_products, n_row, n_col),
        head + [right_sides] + z + y, [SMEM], [narrow] * (n_row + n_col), work,
    )
    y = send_all(rest[n_row - 1 :], "col")
    z = send_all(rest[: n_row - 1], "row")
    base = [right_sides] + collect(copied, "depth")
    (image,) = call(functools.partial(first_combine, n_row, n_col), [partial] + z + y, [], [narrow], [])
    z = send_all([image] * (n_row - 1), "row")
    (image_wide,) = call(functools.partial(first_grams, n_depth), [image] + base, [], [wide], [fields])
    y = send_all([image_wide] * (n_col - 1), "col")
    image = [image] + collect(image, "depth")
    partial, gram, *rest = call(
        functools.partial(second_products, n_row, n_col),
        head + [image_wide] + z + y, [SMEM],
        [narrow, tail] + [wide] * (n_row - 1) + [narrow] * (n_col - 1), work,
    )
    y = send_all(rest[n_row - 1 :], "col")
    z = send_all(rest[: n_row - 1], "row")
    n_all = n_row * n_col * n_depth
    mapped, late = call(
        functools.partial(second_combine, n_row, n_col, n_depth),
        [partial, gram] + z + y + base + image, [], [wide, (n_all,) + tail], [fields],
    )
    mapped = [mapped] + collect(mapped, "depth")
    late = lax.all_to_all(late, ("row", "col", "depth"), 0, 0)
    solved = call(
        functools.partial(early_solve, n_depth, points), mapped, [],
        [square, (size, width), (size, width)], [pltpu.VMEM(square, f32)],
        pl.CostEstimate(flops=4 * size**3, transcendentals=0, bytes_accessed=160 * size * size),
    )
    solution, residual = call(
        functools.partial(finish, n_depth),
        [late] + list(solved) + mapped + base + image, [], [narrow, narrow], [fields, fields, fields],
    )
    return solution, residual


def solution(mesh):
    return jax.shard_map(
        per_device,
        mesh=mesh,
        in_specs=(
            P("depth", ("row", "col")),
            P("row", "col", None, None, None),
            P("row", "col", None),
            P("row", "col", None),
            P("row", "col"),
        ),
        out_specs=(P("depth", ("row", "col")), P("depth", ("row", "col"))),
        check_vma=False,
    )
```

```python
import functools

import jax
import jax.numpy as jnp
from jax import lax
from jax.experimental import pallas as pl
from jax.experimental.pallas import tpu as pltpu
from jax.sharding import PartitionSpec as P


BLK = 256
SEG = 2
PIVOT = 4
HIGHEST = lax.Precision.HIGHEST
VMEM = pl.BlockSpec(memory_space=pltpu.VMEM)
SMEM = pl.BlockSpec(memory_space=pltpu.SMEM)
PARAMS = pltpu.CompilerParams(vmem_limit_bytes=40 << 20)


def partner(index, step, size):
    return index ^ step if size & (size - 1) == 0 else (index + step) % size


def power_of_two(n):
    return n & (n - 1) == 0


def send_all(arrays, axis):
    size = lax.axis_size(axis)
    return [send(arrays[k - 1], axis, k) for k in range(1, size)]


def send(x, axis, step):
    size = lax.axis_size(axis)
    return lax.ppermute(x, axis, [(i, partner(i, step, size)) for i in range(size)])


def collect(x, axis):
    size = lax.axis_size(axis)
    if not power_of_two(size):
        return send_all([x] * (size - 1), axis)
    held = {0: x}
    for k in sorted(range(1, size), key=lambda k: (k.bit_count(), -k)):
        low = k & -k
        held[k] = send(held[k - low], axis, low)
    return [held[k] for k in range(1, size)]


def source_of(axis, step):
    index, size = lax.axis_index(axis), lax.axis_size(axis)
    if size & (size - 1) == 0:
        return index ^ step
    return lax.rem(index + size - step, size)


def partner_of(axis, step):
    index, size = lax.axis_index(axis), lax.axis_size(axis)
    if size & (size - 1) == 0:
        return index ^ step
    return lax.rem(index + step, size)


def dot_nt(a, b):
    return lax.dot_general(a, b, (((1,), (1,)), ((), ())), precision=HIGHEST, preferred_element_type=jnp.float32)


def dot_tn(a, b):
    return lax.dot_general(a, b, (((0,), (0,)), ((), ())), precision=HIGHEST, preferred_element_type=jnp.float32)


def dot_nn(a, b):
    return lax.dot_general(a, b, (((1,), (0,)), ((), ())), precision=HIGHEST, preferred_element_type=jnp.float32)


def halves(x):
    high = x.astype(jnp.bfloat16)
    return high, (x - high.astype(jnp.float32)).astype(jnp.bfloat16)


def bf16_dot(a, b, contract):
    return lax.dot_general(a, b, (contract, ((), ())), preferred_element_type=jnp.float32)


def stack_fields(all_ref, own_ref, depth_refs):
    width, points = own_ref.shape[0], all_ref.shape[1]
    for step, ref in enumerate([own_ref] + depth_refs):
        place = source_of("depth", step)
        all_ref[pl.ds(pl.multiple_of(place * width, width), width), :] = ref[:, 0:points]


def prepare(count_ref, rows_ref, cols_ref, blocks_ref, blocks_out, table_out, rows_at, cols_at, sems):
    slots = blocks_ref.shape[2]
    copies = [pltpu.make_async_copy(blocks_ref.at[0, 0, s], blocks_out.at[s], sems.at[s]) for s in range(slots)]
    small = [
        pltpu.make_async_copy(rows_ref, rows_at, sems.at[slots]),
        pltpu.make_async_copy(cols_ref, cols_at, sems.at[slots + 1]),
    ]
    for copy in small + copies:
        copy.start()
    for copy in small:
        copy.wait()
    for slot in range(slots):
        table_out[0, slot] = rows_at[0, 0, slot]
        table_out[1, slot] = cols_at[0, 0, slot]
        table_out[2, slot] = count_ref[0, 0]
    for copy in copies:
        copy.wait()


def products(
    table_ref, blocks_ref, own_ref, z_refs, y_refs, own_out, z_outs, y_outs,
    col_in, row_in, col_acc, row_acc,
):
    width = own_ref.shape[0]
    row_at, col_at = lax.axis_index("row"), lax.axis_index("col")
    for axis, refs, held in (("row", [own_ref] + z_refs, col_in), ("col", [own_ref] + y_refs, row_in)):
        for step, ref in enumerate(refs):
            place = source_of(axis, step)
            for part in range(SEG):
                high, low = halves(ref[:, part * BLK : (part + 1) * BLK])
                held[place * SEG + part] = jnp.concatenate([high, low], axis=0)
    col_acc[...] = jnp.zeros_like(col_acc)
    row_acc[...] = jnp.zeros_like(row_acc)
    count = table_ref[2, 0]
    for slot in range(blocks_ref.shape[0]):
        high, low = halves(blocks_ref[slot])
        row_place, col_place = table_ref[0, slot], table_ref[1, slot]
        live = slot < count
        for vec, acc, at_in, at_out, contract in (
            (col_in, row_acc, col_place, row_place, ((1,), (1,))),
            (row_in, col_acc, row_place, col_place, ((1,), (0,))),
        ):
            if slot < SEG and acc is col_acc:
                continue
            both = vec[at_in]
            wide = bf16_dot(both, high, contract)
            term = wide[:width] + wide[width:] + bf16_dot(both[:width], low, contract)
            acc[at_out] += jnp.where(live, term, 0.0)
    for part in range(SEG):
        lanes = slice(part * BLK, (part + 1) * BLK)
        own_out[:, lanes] = row_acc[col_at * SEG + part] + col_acc[row_at * SEG + part]
        for step, ref in enumerate(z_outs, 1):
            ref[:, lanes] = col_acc[partner_of("row", step) * SEG + part]
        for step, ref in enumerate(y_outs, 1):
            ref[:, lanes] = row_acc[partner_of("col", step) * SEG + part]


def split(refs, *sizes):
    out = []
    for size in sizes:
        out.append(list(refs[:size]))
        refs = refs[size:]
    return out


def first_products(n_row, n_col, *refs):
    (head, own, z_in, y_in, outs, z_outs, y_outs, scratch) = split(
        refs, 2, 1, n_row - 1, n_col - 1, 2, n_row - 1, n_col - 1, 4
    )
    outs[1][...] = own[0][...]
    products(*head, own[0], z_in, y_in, outs[0], z_outs, y_outs, *scratch)


def first_combine(n_row, n_col, *refs):
    partial, received, out = split(refs, 1, n_row + n_col - 2, 1)
    total = partial[0][...]
    for ref in received:
        total += ref[...]
    out[0][...] = total


def first_grams(n_depth, *refs):
    image, field_refs, out, fields = split(refs, 1, n_depth, 1, 1)
    total = image[0][...]
    points = total.shape[1]
    stack_fields(fields[0], field_refs[0], field_refs[1:])
    everything = fields[0][...]
    out[0][:, :points] = total
    out[0][:, points:] = jnp.concatenate(
        [dot_nt(field_refs[0][...], everything), dot_nt(total, everything)], axis=1
    )


def second_products(n_row, n_col, *refs):
    (head, own, z_in, y_in, outs, z_outs, y_outs, scratch) = split(
        refs, 2, 1, n_row - 1, n_col - 1, 2, n_row - 1, n_col - 1, 4
    )
    points = outs[0].shape[1]
    products(*head, own[0], z_in, y_in, outs[0], z_outs, y_outs, *scratch)
    grams = own[0][:, points:]
    for ref in y_in:
        grams += ref[:, points:]
    outs[1][...] = grams
    for ref in z_outs:
        ref[:, points:] = grams


def second_combine(n_row, n_col, n_depth, *refs):
    partial, gram, z_in, y_in, base_refs, image_refs, out_wide, out_gram, fields = split(
        refs, 1, 1, n_row - 1, n_col - 1, n_depth, n_depth, 1, 1, 1
    )
    points = partial[0].shape[1]
    total = partial[0][...]
    early = gram[0][...]
    for ref in z_in:
        total += ref[:, :points]
        early += ref[:, points:]
    for ref in y_in:
        total += ref[...]
    out_wide[0][:, :points] = total
    out_wide[0][:, points:] = early
    stack_fields(fields[0], base_refs[0], base_refs[1:])
    third = dot_nt(total, fields[0][...])
    stack_fields(fields[0], image_refs[0], image_refs[1:])
    fourth = dot_nt(total, fields[0][...])
    late = jnp.concatenate([third, fourth], axis=1)
    for i in range(out_gram[0].shape[0]):
        out_gram[0][i] = late


def factor_two(e):
    a, b, d = e(0, 0), e(0, 1), e(1, 1)
    scale = 1.0 / (a * d - b * b)
    a, b, d = a * scale, b * scale, d * scale
    return lambda q: [d * q[0] - b * q[1], a * q[1] - b * q[0]]


def factor(e, size):
    if size == 2:
        return factor_two(e)
    half = size // 2
    top = factor(e, half)
    columns = [top([e(i, half + j) for i in range(half)]) for j in range(half)]

    def schur(i, j):
        return e(half + i, half + j) - sum(e(a, half + i) * columns[j][a] for a in range(half))

    entries = {(i, j): schur(i, j) for i in range(half) for j in range(i, half)}
    bottom = factor(lambda i, j: entries[i, j], half)

    def solve(q):
        upper = top(q[:half])
        lower = bottom([q[half + i] - sum(columns[i][a] * q[a] for a in range(half)) for i in range(half)])
        return [upper[a] - sum(columns[i][a] * lower[i] for i in range(half)) for a in range(half)] + lower

    return solve


def eliminate(tables, pivot):
    size, wide = tables[0].shape
    sub = 8
    at_row = lax.broadcasted_iota(jnp.int32, (sub, wide), 0)
    one = tables[0][:sub] * 0.0 + 1.0
    tables = [[table[t : t + sub] for t in range(0, size, sub)] for table in tables]
    for k in range(0, size, pivot):
        home, base = k // sub, k % sub
        for tiles in tables:
            spread = [
                [jnp.broadcast_to(tile[:, k + j : k + j + 1], (sub, wide)) for tile in tiles] for j in range(pivot)
            ]
            row = [jnp.broadcast_to(tiles[home][base + i : base + i + 1], (sub, wide)) for i in range(pivot)]
            near = [spread[j][home] * one for j in range(pivot)]
            entries = {
                (i, j): jnp.broadcast_to(near[j][base + i : base + i + 1], (sub, wide))
                for j in range(pivot)
                for i in range(j + 1)
            }
            solved = factor(lambda i, j: entries[i, j], pivot)(row)
            for t, tile in enumerate(tiles):
                if t == home and pivot == sub:
                    tiles[t] = solved[0]
                else:
                    tiles[t] = tile - sum(spread[j][t] * solved[j] for j in range(pivot))
                if t == home:
                    for i in range(pivot):
                        tiles[t] = jnp.where(at_row == base + i, solved[i], tiles[t])
    return [jnp.concatenate(tiles, axis=0) for tiles in tables]


def identity_of(size):
    shape = (size, size)
    same = lax.broadcasted_iota(jnp.int32, shape, 0) == lax.broadcasted_iota(jnp.int32, shape, 1)
    return same.astype(jnp.float32)


def early_solve(n_depth, points, *refs):
    wide_refs, outs, scratch = split(refs, n_depth, 3, 1)
    width = wide_refs[0].shape[0]
    size = n_depth * width
    for step, ref in enumerate(wide_refs):
        place = source_of("depth", step)
        scratch[0][pl.ds(pl.multiple_of(place * width, width), width), :] = ref[:, points + size : points + 2 * size]
    gram1 = scratch[0][...]
    (first,) = eliminate([jnp.concatenate([gram1, identity_of(size)], axis=1)], PIVOT)
    inverse = first[:, size:]
    outs[0][...] = inverse
    outs[1][...] = dot_nt(inverse, wide_refs[0][:, points : points + size])
    outs[2][...] = dot_nt(identity_of(size), wide_refs[0][:, points + size : points + 2 * size])


def finish(n_depth, *refs):
    gathered, solved, wide_refs, base_refs, image_refs, outs, scratch = split(
        refs, 1, 3, n_depth, n_depth, n_depth, 2, 3
    )
    base, image, mapped = scratch
    solution_out, residual_out = outs
    width, _ = solution_out.shape
    size = n_depth * width
    groups = gathered[0].shape[0] // n_depth
    stack_fields(base, base_refs[0], base_refs[1:])
    stack_fields(image, image_refs[0], image_refs[1:])
    stack_fields(mapped, wide_refs[0], wide_refs[1:])
    late = [sum(gathered[0][g * n_depth + d] for g in range(groups)) for d in range(n_depth)]
    late = jnp.concatenate(late, axis=0)
    gram2, gram3 = late[:, :size], late[:, size:]
    inverse, start, gram1_own = (ref[...] for ref in solved)
    carry = dot_nn(inverse, gram2)
    schur = gram3 - dot_nn(gram2, carry)
    right = gram1_own - dot_nn(gram2, start)
    fill = jnp.zeros((size, size - width), jnp.float32)
    (second,) = eliminate([jnp.concatenate([schur, right, fill], axis=1)], PIVOT)
    weight1 = second[:, size : size + width]
    weight0 = start - dot_nn(carry, weight1)
    base_all, image_all = base[...], image[...]
    solution_out[...] = dot_tn(weight0, base_all) + dot_tn(weight1, image_all)
    residual_out[...] = base_refs[0][...] - dot_tn(weight0, image_all) - dot_tn(weight1, mapped[...])


def call(body, operands, in_specs, out_shapes, scratch, cost=None, out_specs=None):
    return pl.pallas_call(
        body,
        out_shape=[s if hasattr(s, "dtype") else jax.ShapeDtypeStruct(s, jnp.float32) for s in out_shapes],
        in_specs=list(in_specs) + [VMEM] * (len(operands) - len(in_specs)),
        out_specs=out_specs or [VMEM] * len(out_shapes),
        scratch_shapes=scratch,
        compiler_params=PARAMS,
        cost_estimate=cost,
    )(*operands)


def per_device(right_sides, blocks, block_rows, block_cols, block_count):
    n_row, n_col, n_depth = (lax.axis_size(a) for a in ("row", "col", "depth"))
    width, points = right_sides.shape
    size = n_depth * width
    slots = blocks.shape[2]
    f32, b16 = jnp.float32, jnp.bfloat16
    work = [
        pltpu.VMEM((n_row * SEG, 2 * width, BLK), b16),
        pltpu.VMEM((n_col * SEG, 2 * width, BLK), b16),
        pltpu.VMEM((n_row * SEG, width, BLK), f32),
        pltpu.VMEM((n_col * SEG, width, BLK), f32),
    ]
    fields = pltpu.VMEM((size, points), f32)
    narrow, wide, tail, square = (width, points), (width, points + 2 * size), (width, 2 * size), (size, size)

    y = send_all([right_sides] * (n_col - 1), "col")
    z = send_all([right_sides] * (n_row - 1), "row")
    near, table = call(
        prepare,
        [block_count] + [pltpu.with_memory_space_constraint(x, pltpu.HBM) for x in (block_rows, block_cols, blocks)],
        [SMEM] + [pl.BlockSpec(memory_space=pltpu.HBM)] * 3,
        [blocks.shape[2:], jax.ShapeDtypeStruct((3, slots), jnp.int32)],
        [pltpu.SMEM(block_rows.shape, jnp.int32)] * 2 + [pltpu.SemaphoreType.DMA((slots + 2,))],
        pl.CostEstimate(flops=0, transcendentals=0, bytes_accessed=8 * blocks.size),
        [VMEM, SMEM],
    )
    head = [table, near]
    partial, copied, *rest = call(
        functools.partial(first_products, n_row, n_col),
        head + [right_sides] + z + y, [SMEM], [narrow] * (n_row + n_col), work,
    )
    y = send_all(rest[n_row - 1 :], "col")
    z = send_all(rest[: n_row - 1], "row")
    base = [right_sides] + collect(copied, "depth")
    (image,) = call(functools.partial(first_combine, n_row, n_col), [partial] + z + y, [], [narrow], [])
    z = send_all([image] * (n_row - 1), "row")
    (image_wide,) = call(functools.partial(first_grams, n_depth), [image] + base, [], [wide], [fields])
    y = send_all([image_wide] * (n_col - 1), "col")
    image = [image] + collect(image, "depth")
    partial, gram, *rest = call(
        functools.partial(second_products, n_row, n_col),
        head + [image_wide] + z + y, [SMEM],
        [narrow, tail] + [wide] * (n_row - 1) + [narrow] * (n_col - 1), work,
    )
    y = send_all(rest[n_row - 1 :], "col")
    z = send_all(rest[: n_row - 1], "row")
    n_all = n_row * n_col * n_depth
    mapped, late = call(
        functools.partial(second_combine, n_row, n_col, n_depth),
        [partial, gram] + z + y + base + image, [], [wide, (n_all,) + tail], [fields],
    )
    mapped = [mapped] + collect(mapped, "depth")
    late = lax.all_to_all(late, ("row", "col", "depth"), 0, 0)
    solved = call(
        functools.partial(early_solve, n_depth, points), mapped, [],
        [square, (size, width), (size, width)], [pltpu.VMEM(square, f32)],
        pl.CostEstimate(flops=4 * size**3, transcendentals=0, bytes_accessed=160 * size * size),
    )
    solution, residual = call(
        functools.partial(finish, n_depth),
        [late] + list(solved) + mapped + base + image, [], [narrow, narrow], [fields, fields, fields],
    )
    return solution, residual


def solution(mesh):
    return jax.shard_map(
        per_device,
        mesh=mesh,
        in_specs=(
            P("depth", ("row", "col")),
            P("row", "col", None, None, None),
            P("row", "col", None),
            P("row", "col", None),
            P("row", "col"),
        ),
        out_specs=(P("depth", ("row", "col")), P("depth", ("row", "col"))),
        check_vma=False,
    )
```

```python
import functools

import jax
import jax.numpy as jnp
from jax import lax
from jax.experimental import pallas as pl
from jax.experimental.pallas import tpu as pltpu
from jax.sharding import PartitionSpec as P


BLK = 256
SEG = 2
PIVOT = 4
HIGHEST = lax.Precision.HIGHEST
VMEM = pl.BlockSpec(memory_space=pltpu.VMEM)
SMEM = pl.BlockSpec(memory_space=pltpu.SMEM)
PARAMS = pltpu.CompilerParams(vmem_limit_bytes=40 << 20)


def partner(index, step, size):
    return index ^ step if size & (size - 1) == 0 else (index + step) % size


def power_of_two(n):
    return n & (n - 1) == 0


def send_all(arrays, axis):
    size = lax.axis_size(axis)
    return [send(arrays[k - 1], axis, k) for k in range(1, size)]


def send(x, axis, step):
    size = lax.axis_size(axis)
    return lax.ppermute(x, axis, [(i, partner(i, step, size)) for i in range(size)])


def collect(x, axis):
    size = lax.axis_size(axis)
    if not power_of_two(size):
        return send_all([x] * (size - 1), axis)
    held = {0: x}
    for k in sorted(range(1, size), key=lambda k: (k.bit_count(), -k)):
        low = k & -k
        held[k] = send(held[k - low], axis, low)
    return [held[k] for k in range(1, size)]


def source_of(axis, step):
    index, size = lax.axis_index(axis), lax.axis_size(axis)
    if size & (size - 1) == 0:
        return index ^ step
    return lax.rem(index + size - step, size)


def partner_of(axis, step):
    index, size = lax.axis_index(axis), lax.axis_size(axis)
    if size & (size - 1) == 0:
        return index ^ step
    return lax.rem(index + step, size)


def dot_nt(a, b):
    return lax.dot_general(a, b, (((1,), (1,)), ((), ())), precision=HIGHEST, preferred_element_type=jnp.float32)


def dot_tn(a, b):
    return lax.dot_general(a, b, (((0,), (0,)), ((), ())), precision=HIGHEST, preferred_element_type=jnp.float32)


def dot_nn(a, b):
    return lax.dot_general(a, b, (((1,), (0,)), ((), ())), precision=HIGHEST, preferred_element_type=jnp.float32)


def halves(x):
    high = x.astype(jnp.bfloat16)
    return high, (x - high.astype(jnp.float32)).astype(jnp.bfloat16)


def bf16_dot(a, b, contract):
    return lax.dot_general(a, b, (contract, ((), ())), preferred_element_type=jnp.float32)


def stack_fields(all_ref, own_ref, depth_refs):
    width, points = own_ref.shape[0], all_ref.shape[1]
    for step, ref in enumerate([own_ref] + depth_refs):
        place = source_of("depth", step)
        all_ref[pl.ds(pl.multiple_of(place * width, width), width), :] = ref[:, 0:points]


def prepare(count_ref, rows_ref, cols_ref, blocks_ref, blocks_out, table_out, rows_at, cols_at, sems):
    slots = blocks_ref.shape[2]
    copies = [pltpu.make_async_copy(blocks_ref.at[0, 0, s], blocks_out.at[s], sems.at[s]) for s in range(slots)]
    small = [
        pltpu.make_async_copy(rows_ref, rows_at, sems.at[slots]),
        pltpu.make_async_copy(cols_ref, cols_at, sems.at[slots + 1]),
    ]
    for copy in small + copies:
        copy.start()
    for copy in small:
        copy.wait()
    for slot in range(slots):
        table_out[0, slot] = rows_at[0, 0, slot]
        table_out[1, slot] = cols_at[0, 0, slot]
        table_out[2, slot] = count_ref[0, 0]
    for copy in copies:
        copy.wait()


def products(
    table_ref, blocks_ref, own_ref, z_refs, y_refs, own_out, z_outs, y_outs,
    col_in, row_in, col_acc, row_acc,
):
    width = own_ref.shape[0]
    row_at, col_at = lax.axis_index("row"), lax.axis_index("col")
    for axis, refs, held in (("row", [own_ref] + z_refs, col_in), ("col", [own_ref] + y_refs, row_in)):
        for step, ref in enumerate(refs):
            place = source_of(axis, step)
            for part in range(SEG):
                high, low = halves(ref[:, part * BLK : (part + 1) * BLK])
                held[place * SEG + part] = jnp.concatenate([high, low], axis=0)
    col_acc[...] = jnp.zeros_like(col_acc)
    row_acc[...] = jnp.zeros_like(row_acc)
    count = table_ref[2, 0]
    for slot in range(blocks_ref.shape[0]):
        high, low = halves(blocks_ref[slot])
        row_place, col_place = table_ref[0, slot], table_ref[1, slot]
        live = slot < count
        for vec, acc, at_in, at_out, contract in (
            (col_in, row_acc, col_place, row_place, ((1,), (1,))),
            (row_in, col_acc, row_place, col_place, ((1,), (0,))),
        ):
            if slot < SEG and acc is col_acc:
                continue
            both = vec[at_in]
            wide = bf16_dot(both, high, contract)
            term = wide[:width] + wide[width:] + bf16_dot(both[:width], low, contract)
            acc[at_out] += jnp.where(live, term, 0.0)
    for part in range(SEG):
        lanes = slice(part * BLK, (part + 1) * BLK)
        own_out[:, lanes] = row_acc[col_at * SEG + part] + col_acc[row_at * SEG + part]
        for step, ref in enumerate(z_outs, 1):
            ref[:, lanes] = col_acc[partner_of("row", step) * SEG + part]
        for step, ref in enumerate(y_outs, 1):
            ref[:, lanes] = row_acc[partner_of("col", step) * SEG + part]


def split(refs, *sizes):
    out = []
    for size in sizes:
        out.append(list(refs[:size]))
        refs = refs[size:]
    return out


def first_products(n_row, n_col, *refs):
    (head, own, z_in, y_in, outs, z_outs, y_outs, scratch) = split(
        refs, 2, 1, n_row - 1, n_col - 1, 2, n_row - 1, n_col - 1, 4
    )
    outs[1][...] = own[0][...]
    products(*head, own[0], z_in, y_in, outs[0], z_outs, y_outs, *scratch)


def first_combine(n_row, n_col, *refs):
    partial, received, out = split(refs, 1, n_row + n_col - 2, 1)
    total = partial[0][...]
    for ref in received:
        total += ref[...]
    out[0][...] = total


def first_grams(n_depth, *refs):
    image, field_refs, out, fields = split(refs, 1, n_depth, 1, 1)
    total = image[0][...]
    points = total.shape[1]
    stack_fields(fields[0], field_refs[0], field_refs[1:])
    everything = fields[0][...]
    out[0][:, :points] = total
    out[0][:, points:] = jnp.concatenate(
        [dot_nt(field_refs[0][...], everything), dot_nt(total, everything)], axis=1
    )


def second_products(n_row, n_col, *refs):
    (head, own, z_in, y_in, outs, z_outs, y_outs, scratch) = split(
        refs, 2, 1, n_row - 1, n_col - 1, 2, n_row - 1, n_col - 1, 4
    )
    points = outs[0].shape[1]
    products(*head, own[0], z_in, y_in, outs[0], z_outs, y_outs, *scratch)
    grams = own[0][:, points:]
    for ref in y_in:
        grams += ref[:, points:]
    outs[1][...] = grams
    for ref in z_outs:
        ref[:, points:] = grams


def second_combine(n_row, n_col, n_depth, *refs):
    partial, gram, z_in, y_in, base_refs, image_refs, out_wide, out_gram, fields = split(
        refs, 1, 1, n_row - 1, n_col - 1, n_depth, n_depth, 1, 1, 1
    )
    points = partial[0].shape[1]
    total = partial[0][...]
    early = gram[0][...]
    for ref in z_in:
        total += ref[:, :points]
        early += ref[:, points:]
    for ref in y_in:
        total += ref[...]
    out_wide[0][:, :points] = total
    out_wide[0][:, points:] = early
    stack_fields(fields[0], base_refs[0], base_refs[1:])
    third = dot_nt(total, fields[0][...])
    stack_fields(fields[0], image_refs[0], image_refs[1:])
    fourth = dot_nt(total, fields[0][...])
    width = total.shape[0]
    packed = [jnp.concatenate([g[: width // 2], g[width // 2 :]], axis=1) for g in (third, fourth)]
    for i in range(out_gram[0].shape[0]):
        out_gram[0][i] = packed[i % n_depth % 2]


def factor_two(e):
    a, b, d = e(0, 0), e(0, 1), e(1, 1)
    scale = 1.0 / (a * d - b * b)
    a, b, d = a * scale, b * scale, d * scale
    return lambda q: [d * q[0] - b * q[1], a * q[1] - b * q[0]]


def factor(e, size):
    if size == 2:
        return factor_two(e)
    half = size // 2
    top = factor(e, half)
    columns = [top([e(i, half + j) for i in range(half)]) for j in range(half)]

    def schur(i, j):
        return e(half + i, half + j) - sum(e(a, half + i) * columns[j][a] for a in range(half))

    entries = {(i, j): schur(i, j) for i in range(half) for j in range(i, half)}
    bottom = factor(lambda i, j: entries[i, j], half)

    def solve(q):
        upper = top(q[:half])
        lower = bottom([q[half + i] - sum(columns[i][a] * q[a] for a in range(half)) for i in range(half)])
        return [upper[a] - sum(columns[i][a] * lower[i] for i in range(half)) for a in range(half)] + lower

    return solve


def eliminate(tables, pivot):
    size, wide = tables[0].shape
    sub = 8
    at_row = lax.broadcasted_iota(jnp.int32, (sub, wide), 0)
    one = tables[0][:sub] * 0.0 + 1.0
    tables = [[table[t : t + sub] for t in range(0, size, sub)] for table in tables]
    for k in range(0, size, pivot):
        home, base = k // sub, k % sub
        for tiles in tables:
            spread = [
                [jnp.broadcast_to(tile[:, k + j : k + j + 1], (sub, wide)) for tile in tiles] for j in range(pivot)
            ]
            row = [jnp.broadcast_to(tiles[home][base + i : base + i + 1], (sub, wide)) for i in range(pivot)]
            near = [spread[j][home] * one for j in range(pivot)]
            entries = {
                (i, j): jnp.broadcast_to(near[j][base + i : base + i + 1], (sub, wide))
                for j in range(pivot)
                for i in range(j + 1)
            }
            solved = factor(lambda i, j: entries[i, j], pivot)(row)
            for t, tile in enumerate(tiles):
                if t == home and pivot == sub:
                    tiles[t] = solved[0]
                else:
                    tiles[t] = tile - sum(spread[j][t] * solved[j] for j in range(pivot))
                if t == home:
                    for i in range(pivot):
                        tiles[t] = jnp.where(at_row == base + i, solved[i], tiles[t])
    return [jnp.concatenate(tiles, axis=0) for tiles in tables]


def identity_of(size):
    shape = (size, size)
    same = lax.broadcasted_iota(jnp.int32, shape, 0) == lax.broadcasted_iota(jnp.int32, shape, 1)
    return same.astype(jnp.float32)


def early_solve(n_depth, points, *refs):
    wide_refs, outs, scratch = split(refs, n_depth, 3, 1)
    width = wide_refs[0].shape[0]
    size = n_depth * width
    for step, ref in enumerate(wide_refs):
        place = source_of("depth", step)
        scratch[0][pl.ds(pl.multiple_of(place * width, width), width), :] = ref[:, points + size : points + 2 * size]
    gram1 = scratch[0][...]
    (first,) = eliminate([jnp.concatenate([gram1, identity_of(size)], axis=1)], PIVOT)
    inverse = first[:, size:]
    outs[0][...] = inverse
    outs[1][...] = dot_nt(inverse, wide_refs[0][:, points : points + size])
    outs[2][...] = dot_nt(identity_of(size), wide_refs[0][:, points + size : points + 2 * size])


def late_total(n_depth, gathered_ref, out_ref):
    rows = gathered_ref.shape[1]
    groups = gathered_ref.shape[0] // n_depth
    for d in range(n_depth):
        out_ref[d * rows : (d + 1) * rows, :] = sum(gathered_ref[g * n_depth + d] for g in range(groups))


def unpacked(packed, rows):
    size = packed.shape[1] // 2
    parts = []
    for at in range(0, packed.shape[0], rows):
        part = packed[at : at + rows]
        parts += [part[:, :size], part[:, size:]]
    return jnp.concatenate(parts, axis=0)


def finish(n_depth, *refs):
    late, solved, wide_refs, base_refs, image_refs, outs, scratch = split(
        refs, 2, 3, n_depth, n_depth, n_depth, 2, 3
    )
    base, image, mapped = scratch
    solution_out, residual_out = outs
    width, _ = solution_out.shape
    size = n_depth * width
    stack_fields(base, base_refs[0], base_refs[1:])
    stack_fields(image, image_refs[0], image_refs[1:])
    stack_fields(mapped, wide_refs[0], wide_refs[1:])
    mine, other = (unpacked(ref[...], width // 2) for ref in late)
    even = lax.axis_index("depth") % 2 == 0
    gram2, gram3 = jnp.where(even, mine, other), jnp.where(even, other, mine)
    inverse, start, gram1_own = (ref[...] for ref in solved)
    carry = dot_nn(inverse, gram2)
    schur = gram3 - dot_nn(gram2, carry)
    right = gram1_own - dot_nn(gram2, start)
    fill = jnp.zeros((size, size - width), jnp.float32)
    (second,) = eliminate([jnp.concatenate([schur, right, fill], axis=1)], PIVOT)
    weight1 = second[:, size : size + width]
    weight0 = start - dot_nn(carry, weight1)
    base_all, image_all = base[...], image[...]
    solution_out[...] = dot_tn(weight0, base_all) + dot_tn(weight1, image_all)
    residual_out[...] = base_refs[0][...] - dot_tn(weight0, image_all) - dot_tn(weight1, mapped[...])


def call(body, operands, in_specs, out_shapes, scratch, cost=None, out_specs=None):
    return pl.pallas_call(
        body,
        out_shape=[s if hasattr(s, "dtype") else jax.ShapeDtypeStruct(s, jnp.float32) for s in out_shapes],
        in_specs=list(in_specs) + [VMEM] * (len(operands) - len(in_specs)),
        out_specs=out_specs or [VMEM] * len(out_shapes),
        scratch_shapes=scratch,
        compiler_params=PARAMS,
        cost_estimate=cost,
    )(*operands)


def per_device(right_sides, blocks, block_rows, block_cols, block_count):
    n_row, n_col, n_depth = (lax.axis_size(a) for a in ("row", "col", "depth"))
    width, points = right_sides.shape
    size = n_depth * width
    slots = blocks.shape[2]
    f32, b16 = jnp.float32, jnp.bfloat16
    work = [
        pltpu.VMEM((n_row * SEG, 2 * width, BLK), b16),
        pltpu.VMEM((n_col * SEG, 2 * width, BLK), b16),
        pltpu.VMEM((n_row * SEG, width, BLK), f32),
        pltpu.VMEM((n_col * SEG, width, BLK), f32),
    ]
    fields = pltpu.VMEM((size, points), f32)
    narrow, wide, tail, square = (width, points), (width, points + 2 * size), (width, 2 * size), (size, size)

    y = send_all([right_sides] * (n_col - 1), "col")
    z = send_all([right_sides] * (n_row - 1), "row")
    near, table = call(
        prepare,
        [block_count] + [pltpu.with_memory_space_constraint(x, pltpu.HBM) for x in (block_rows, block_cols, blocks)],
        [SMEM] + [pl.BlockSpec(memory_space=pltpu.HBM)] * 3,
        [blocks.shape[2:], jax.ShapeDtypeStruct((3, slots), jnp.int32)],
        [pltpu.SMEM(block_rows.shape, jnp.int32)] * 2 + [pltpu.SemaphoreType.DMA((slots + 2,))],
        pl.CostEstimate(flops=0, transcendentals=0, bytes_accessed=8 * blocks.size),
        [VMEM, SMEM],
    )
    head = [table, near]
    partial, copied, *rest = call(
        functools.partial(first_products, n_row, n_col),
        head + [right_sides] + z + y, [SMEM], [narrow] * (n_row + n_col), work,
    )
    y = send_all(rest[n_row - 1 :], "col")
    z = send_all(rest[: n_row - 1], "row")
    base = [right_sides] + collect(copied, "depth")
    (image,) = call(functools.partial(first_combine, n_row, n_col), [partial] + z + y, [], [narrow], [])
    z = send_all([image] * (n_row - 1), "row")
    (image_wide,) = call(functools.partial(first_grams, n_depth), [image] + base, [], [wide], [fields])
    y = send_all([image_wide] * (n_col - 1), "col")
    image = [image] + collect(image, "depth")
    partial, gram, *rest = call(
        functools.partial(second_products, n_row, n_col),
        head + [image_wide] + z + y, [SMEM],
        [narrow, tail] + [wide] * (n_row - 1) + [narrow] * (n_col - 1), work,
    )
    y = send_all(rest[n_row - 1 :], "col")
    z = send_all(rest[: n_row - 1], "row")
    n_all = n_row * n_col * n_depth
    mapped, late = call(
        functools.partial(second_combine, n_row, n_col, n_depth),
        [partial, gram] + z + y + base + image, [], [wide, (n_all, width // 2, 2 * size)], [fields],
    )
    mapped = [mapped] + collect(mapped, "depth")
    late = lax.all_to_all(late, ("row", "col", "depth"), 0, 0)
    solved = call(
        functools.partial(early_solve, n_depth, points), mapped, [],
        [square, (size, width), (size, width)], [pltpu.VMEM(square, f32)],
        pl.CostEstimate(flops=4 * size**3, transcendentals=0, bytes_accessed=160 * size * size),
    )
    (late,) = call(functools.partial(late_total, n_depth), [late], [], [(size // 2, 2 * size)], [])
    other = lax.ppermute(late, "depth", [(i, i ^ 1) for i in range(n_depth)])
    solution, residual = call(
        functools.partial(finish, n_depth),
        [late, other] + list(solved) + mapped + base + image, [], [narrow, narrow], [fields, fields, fields],
    )
    return solution, residual


def solution(mesh):
    return jax.shard_map(
        per_device,
        mesh=mesh,
        in_specs=(
            P("depth", ("row", "col")),
            P("row", "col", None, None, None),
            P("row", "col", None),
            P("row", "col", None),
            P("row", "col"),
        ),
        out_specs=(P("depth", ("row", "col")), P("depth", ("row", "col"))),
        check_vma=False,
    )
```

```python
import functools

import jax
import jax.numpy as jnp
from jax import lax
from jax.experimental import pallas as pl
from jax.experimental.pallas import tpu as pltpu
from jax.sharding import PartitionSpec as P


BLK = 256
SEG = 2
PIVOT = 8
PANEL = 32
HIGHEST = lax.Precision.HIGHEST
VMEM = pl.BlockSpec(memory_space=pltpu.VMEM)
SMEM = pl.BlockSpec(memory_space=pltpu.SMEM)
PARAMS = pltpu.CompilerParams(vmem_limit_bytes=40 << 20)


def partner(index, step, size):
    return index ^ step if size & (size - 1) == 0 else (index + step) % size


def power_of_two(n):
    return n & (n - 1) == 0


def send_all(arrays, axis):
    size = lax.axis_size(axis)
    return [send(arrays[k - 1], axis, k) for k in range(1, size)]


def send(x, axis, step):
    size = lax.axis_size(axis)
    return lax.ppermute(x, axis, [(i, partner(i, step, size)) for i in range(size)])


def collect(x, axis):
    size = lax.axis_size(axis)
    if not power_of_two(size):
        return send_all([x] * (size - 1), axis)
    held = {0: x}
    for k in sorted(range(1, size), key=lambda k: (k.bit_count(), -k)):
        low = k & -k
        held[k] = send(held[k - low], axis, low)
    return [held[k] for k in range(1, size)]


def source_of(axis, step):
    index, size = lax.axis_index(axis), lax.axis_size(axis)
    if size & (size - 1) == 0:
        return index ^ step
    return lax.rem(index + size - step, size)


def partner_of(axis, step):
    index, size = lax.axis_index(axis), lax.axis_size(axis)
    if size & (size - 1) == 0:
        return index ^ step
    return lax.rem(index + step, size)


def dot_nt(a, b):
    return lax.dot_general(a, b, (((1,), (1,)), ((), ())), precision=HIGHEST, preferred_element_type=jnp.float32)


def dot_tn(a, b):
    return lax.dot_general(a, b, (((0,), (0,)), ((), ())), precision=HIGHEST, preferred_element_type=jnp.float32)


def dot_nn(a, b):
    return lax.dot_general(a, b, (((1,), (0,)), ((), ())), precision=HIGHEST, preferred_element_type=jnp.float32)


def halves(x):
    high = x.astype(jnp.bfloat16)
    return high, (x - high.astype(jnp.float32)).astype(jnp.bfloat16)


def bf16_dot(a, b, contract):
    return lax.dot_general(a, b, (contract, ((), ())), preferred_element_type=jnp.float32)


def stack_fields(all_ref, own_ref, depth_refs):
    width, points = own_ref.shape[0], all_ref.shape[1]
    for step, ref in enumerate([own_ref] + depth_refs):
        place = source_of("depth", step)
        all_ref[pl.ds(pl.multiple_of(place * width, width), width), :] = ref[:, 0:points]


def prepare(count_ref, rows_ref, cols_ref, blocks_ref, blocks_out, table_out, rows_at, cols_at, sems):
    slots = blocks_ref.shape[2]
    copies = [pltpu.make_async_copy(blocks_ref.at[0, 0, s], blocks_out.at[s], sems.at[s]) for s in range(slots)]
    small = [
        pltpu.make_async_copy(rows_ref, rows_at, sems.at[slots]),
        pltpu.make_async_copy(cols_ref, cols_at, sems.at[slots + 1]),
    ]
    for copy in small + copies:
        copy.start()
    for copy in small:
        copy.wait()
    for slot in range(slots):
        table_out[0, slot] = rows_at[0, 0, slot]
        table_out[1, slot] = cols_at[0, 0, slot]
        table_out[2, slot] = count_ref[0, 0]
    for copy in copies:
        copy.wait()


def products(
    table_ref, blocks_ref, own_ref, z_refs, y_refs, own_out, z_outs, y_outs,
    col_in, row_in, col_acc, row_acc,
):
    width = own_ref.shape[0]
    row_at, col_at = lax.axis_index("row"), lax.axis_index("col")
    for axis, refs, held in (("row", [own_ref] + z_refs, col_in), ("col", [own_ref] + y_refs, row_in)):
        for step, ref in enumerate(refs):
            place = source_of(axis, step)
            for part in range(SEG):
                high, low = halves(ref[:, part * BLK : (part + 1) * BLK])
                held[place * SEG + part] = jnp.concatenate([high, low], axis=0)
    col_acc[...] = jnp.zeros_like(col_acc)
    row_acc[...] = jnp.zeros_like(row_acc)
    count = table_ref[2, 0]
    for slot in range(blocks_ref.shape[0]):
        high, low = halves(blocks_ref[slot])
        row_place, col_place = table_ref[0, slot], table_ref[1, slot]
        live = slot < count
        for vec, acc, at_in, at_out, contract in (
            (col_in, row_acc, col_place, row_place, ((1,), (1,))),
            (row_in, col_acc, row_place, col_place, ((1,), (0,))),
        ):
            if slot < SEG and acc is col_acc:
                continue
            both = vec[at_in]
            wide = bf16_dot(both, high, contract)
            term = wide[:width] + wide[width:] + bf16_dot(both[:width], low, contract)
            acc[at_out] += jnp.where(live, term, 0.0)
    for part in range(SEG):
        lanes = slice(part * BLK, (part + 1) * BLK)
        own_out[:, lanes] = row_acc[col_at * SEG + part] + col_acc[row_at * SEG + part]
        for step, ref in enumerate(z_outs, 1):
            ref[:, lanes] = col_acc[partner_of("row", step) * SEG + part]
        for step, ref in enumerate(y_outs, 1):
            ref[:, lanes] = row_acc[partner_of("col", step) * SEG + part]


def split(refs, *sizes):
    out = []
    for size in sizes:
        out.append(list(refs[:size]))
        refs = refs[size:]
    return out


def first_products(n_row, n_col, *refs):
    (head, own, z_in, y_in, outs, z_outs, y_outs, scratch) = split(
        refs, 2, 1, n_row - 1, n_col - 1, 2, n_row - 1, n_col - 1, 4
    )
    outs[1][...] = own[0][...]
    products(*head, own[0], z_in, y_in, outs[0], z_outs, y_outs, *scratch)


def first_combine(n_row, n_col, *refs):
    partial, received, out = split(refs, 1, n_row + n_col - 2, 1)
    total = partial[0][...]
    for ref in received:
        total += ref[...]
    out[0][...] = total


def first_grams(n_depth, *refs):
    image, field_refs, out, fields = split(refs, 1, n_depth, 1, 1)
    total = image[0][...]
    points = total.shape[1]
    stack_fields(fields[0], field_refs[0], field_refs[1:])
    everything = fields[0][...]
    out[0][:, :points] = total
    out[0][:, points:] = jnp.concatenate(
        [dot_nt(field_refs[0][...], everything), dot_nt(total, everything)], axis=1
    )


def second_products(n_row, n_col, *refs):
    (head, own, z_in, y_in, outs, z_outs, y_outs, scratch) = split(
        refs, 2, 1, n_row - 1, n_col - 1, 2, n_row - 1, n_col - 1, 4
    )
    points = outs[0].shape[1]
    products(*head, own[0], z_in, y_in, outs[0], z_outs, y_outs, *scratch)
    grams = own[0][:, points:]
    for ref in y_in:
        grams += ref[:, points:]
    outs[1][...] = grams
    for ref in z_outs:
        ref[:, points:] = grams


def second_combine(n_row, n_col, n_depth, *refs):
    partial, gram, z_in, y_in, base_refs, image_refs, out_wide, out_gram, fields = split(
        refs, 1, 1, n_row - 1, n_col - 1, n_depth, n_depth, 1, 1, 1
    )
    points = partial[0].shape[1]
    total = partial[0][...]
    early = gram[0][...]
    for ref in z_in:
        total += ref[:, :points]
        early += ref[:, points:]
    for ref in y_in:
        total += ref[...]
    out_wide[0][:, :points] = total
    out_wide[0][:, points:] = early
    stack_fields(fields[0], base_refs[0], base_refs[1:])
    third = dot_nt(total, fields[0][...])
    stack_fields(fields[0], image_refs[0], image_refs[1:])
    fourth = dot_nt(total, fields[0][...])
    width = total.shape[0]
    packed = [jnp.concatenate([g[: width // 2], g[width // 2 :]], axis=1) for g in (third, fourth)]
    for i in range(out_gram[0].shape[0]):
        out_gram[0][i] = packed[i % n_depth % 2]


def factor_two(e):
    a, b, d = e(0, 0), e(0, 1), e(1, 1)
    scale = 1.0 / (a * d - b * b)
    a, b, d = a * scale, b * scale, d * scale
    return lambda q: [d * q[0] - b * q[1], a * q[1] - b * q[0]]


def factor(e, size):
    if size == 2:
        return factor_two(e)
    half = size // 2
    top = factor(e, half)
    columns = [top([e(i, half + j) for i in range(half)]) for j in range(half)]

    def schur(i, j):
        return e(half + i, half + j) - sum(e(a, half + i) * columns[j][a] for a in range(half))

    entries = {(i, j): schur(i, j) for i in range(half) for j in range(i, half)}
    bottom = factor(lambda i, j: entries[i, j], half)

    def solve(q):
        upper = top(q[:half])
        lower = bottom([q[half + i] - sum(columns[i][a] * q[a] for a in range(half)) for i in range(half)])
        return [upper[a] - sum(columns[i][a] * lower[i] for i in range(half)) for a in range(half)] + lower

    return solve


def eliminate(table, size, pivot, panel):
    rows, wide = table.shape
    sub = 8
    at_row = lax.broadcasted_iota(jnp.int32, (sub, wide), 0)
    one = table[:sub] * 0.0 + 1.0
    for start in range(0, size, panel):
        stop = start + panel
        tiles = [table[t : t + sub] for t in range(start, stop, sub)]
        for k in range(start, stop, pivot):
            home, base = (k - start) // sub, k % sub
            spread = [
                [jnp.broadcast_to(tile[:, k + j : k + j + 1], (sub, wide)) for tile in tiles] for j in range(pivot)
            ]
            row = [jnp.broadcast_to(tiles[home][base + i : base + i + 1], (sub, wide)) for i in range(pivot)]
            near = [spread[j][home] * one for j in range(pivot)]
            entries = {
                (i, j): jnp.broadcast_to(near[j][base + i : base + i + 1], (sub, wide))
                for j in range(pivot)
                for i in range(j + 1)
            }
            solved = factor(lambda i, j: entries[i, j], pivot)(row)
            for t, tile in enumerate(tiles):
                tiles[t] = tile - sum(spread[j][t] * solved[j] for j in range(pivot))
                if t == home:
                    for i in range(pivot):
                        tiles[t] = jnp.where(at_row == base + i, solved[i], tiles[t])
        done = jnp.concatenate(tiles, axis=0)
        others = [table[at:to] for at, to in ((0, start), (stop, rows)) if at < to]
        others = [part - dot_nn(part[:, start:stop], done) for part in others]
        table = jnp.concatenate(others[:1] + [done] + others[1:] if start else [done] + others, axis=0)
    return table


def identity_of(size):
    shape = (size, size)
    same = lax.broadcasted_iota(jnp.int32, shape, 0) == lax.broadcasted_iota(jnp.int32, shape, 1)
    return same.astype(jnp.float32)


def early_solve(n_depth, points, *refs):
    wide_refs, outs, scratch = split(refs, n_depth, 3, 1)
    width = wide_refs[0].shape[0]
    size = n_depth * width
    for step, ref in enumerate(wide_refs):
        place = source_of("depth", step)
        scratch[0][pl.ds(pl.multiple_of(place * width, width), width), :] = ref[:, points + size : points + 2 * size]
    gram1 = scratch[0][...]
    first = eliminate(jnp.concatenate([gram1, identity_of(size)], axis=1), size, PIVOT, size)
    inverse = first[:, size:]
    outs[0][...] = inverse
    outs[1][...] = dot_nt(inverse, wide_refs[0][:, points : points + size])
    outs[2][...] = dot_nt(identity_of(size), wide_refs[0][:, points + size : points + 2 * size])


def late_total(n_depth, gathered_ref, out_ref):
    rows = gathered_ref.shape[1]
    groups = gathered_ref.shape[0] // n_depth
    for d in range(n_depth):
        out_ref[d * rows : (d + 1) * rows, :] = sum(gathered_ref[g * n_depth + d] for g in range(groups))


def unpacked(packed, rows):
    size = packed.shape[1] // 2
    parts = []
    for at in range(0, packed.shape[0], rows):
        part = packed[at : at + rows]
        parts += [part[:, :size], part[:, size:]]
    return jnp.concatenate(parts, axis=0)


def finish(n_depth, *refs):
    late, solved, wide_refs, base_refs, image_refs, outs, scratch = split(
        refs, 2, 3, n_depth, n_depth, n_depth, 2, 1
    )
    (fields,) = scratch
    solution_out, residual_out = outs
    width, _ = solution_out.shape
    size = n_depth * width
    for i, refs_of in enumerate((base_refs, image_refs, wide_refs)):
        stack_fields(fields.at[i * size : (i + 1) * size], refs_of[0], refs_of[1:])
    mine, other = (unpacked(ref[...], width // 2) for ref in late)
    even = lax.axis_index("depth") % 2 == 0
    gram2, gram3 = jnp.where(even, mine, other), jnp.where(even, other, mine)
    inverse, start, gram1_own = (ref[...] for ref in solved)
    carry = dot_nn(inverse, gram2)
    schur = gram3 - dot_nn(gram2, carry)
    right = gram1_own - dot_nn(gram2, start)
    fill = jnp.zeros((size, size - width), jnp.float32)
    rows = [jnp.concatenate(parts, axis=1) for parts in ((schur, right, fill), (carry, start, fill))]
    weights = eliminate(jnp.concatenate(rows, axis=0), size, PIVOT, PANEL)[:, size : size + width]
    weight1, weight0, none = weights[:size], weights[size:], jnp.zeros((size, width), jnp.float32)
    both = [jnp.concatenate(parts, axis=1) for parts in ((weight0, none), (weight1, weight0), (none, weight1))]
    result = dot_tn(jnp.concatenate(both, axis=0), fields[...])
    solution_out[...] = result[:width]
    residual_out[...] = base_refs[0][...] - result[width:]


def call(body, operands, in_specs, out_shapes, scratch, cost=None, out_specs=None):
    return pl.pallas_call(
        body,
        out_shape=[s if hasattr(s, "dtype") else jax.ShapeDtypeStruct(s, jnp.float32) for s in out_shapes],
        in_specs=list(in_specs) + [VMEM] * (len(operands) - len(in_specs)),
        out_specs=out_specs or [VMEM] * len(out_shapes),
        scratch_shapes=scratch,
        compiler_params=PARAMS,
        cost_estimate=cost,
    )(*operands)


def per_device(right_sides, blocks, block_rows, block_cols, block_count):
    n_row, n_col, n_depth = (lax.axis_size(a) for a in ("row", "col", "depth"))
    width, points = right_sides.shape
    size = n_depth * width
    slots = blocks.shape[2]
    f32, b16 = jnp.float32, jnp.bfloat16
    work = [
        pltpu.VMEM((n_row * SEG, 2 * width, BLK), b16),
        pltpu.VMEM((n_col * SEG, 2 * width, BLK), b16),
        pltpu.VMEM((n_row * SEG, width, BLK), f32),
        pltpu.VMEM((n_col * SEG, width, BLK), f32),
    ]
    fields = pltpu.VMEM((size, points), f32)
    narrow, wide, tail, square = (width, points), (width, points + 2 * size), (width, 2 * size), (size, size)

    y = send_all([right_sides] * (n_col - 1), "col")
    z = send_all([right_sides] * (n_row - 1), "row")
    near, table = call(
        prepare,
        [block_count] + [pltpu.with_memory_space_constraint(x, pltpu.HBM) for x in (block_rows, block_cols, blocks)],
        [SMEM] + [pl.BlockSpec(memory_space=pltpu.HBM)] * 3,
        [blocks.shape[2:], jax.ShapeDtypeStruct((3, slots), jnp.int32)],
        [pltpu.SMEM(block_rows.shape, jnp.int32)] * 2 + [pltpu.SemaphoreType.DMA((slots + 2,))],
        pl.CostEstimate(flops=0, transcendentals=0, bytes_accessed=8 * blocks.size),
        [VMEM, SMEM],
    )
    head = [table, near]
    partial, copied, *rest = call(
        functools.partial(first_products, n_row, n_col),
        head + [right_sides] + z + y, [SMEM], [narrow] * (n_row + n_col), work,
    )
    y = send_all(rest[n_row - 1 :], "col")
    z = send_all(rest[: n_row - 1], "row")
    base = [right_sides] + collect(copied, "depth")
    (image,) = call(functools.partial(first_combine, n_row, n_col), [partial] + z + y, [], [narrow], [])
    z = send_all([image] * (n_row - 1), "row")
    (image_wide,) = call(functools.partial(first_grams, n_depth), [image] + base, [], [wide], [fields])
    y = send_all([image_wide] * (n_col - 1), "col")
    image = [image] + collect(image, "depth")
    partial, gram, *rest = call(
        functools.partial(second_products, n_row, n_col),
        head + [image_wide] + z + y, [SMEM],
        [narrow, tail] + [wide] * (n_row - 1) + [narrow] * (n_col - 1), work,
    )
    y = send_all(rest[n_row - 1 :], "col")
    z = send_all(rest[: n_row - 1], "row")
    n_all = n_row * n_col * n_depth
    mapped, late = call(
        functools.partial(second_combine, n_row, n_col, n_depth),
        [partial, gram] + z + y + base + image, [], [wide, (n_all, width // 2, 2 * size)], [fields],
    )
    mapped = [mapped] + collect(mapped, "depth")
    late = lax.all_to_all(late, ("row", "col", "depth"), 0, 0)
    solved = call(
        functools.partial(early_solve, n_depth, points), mapped, [],
        [square, (size, width), (size, width)], [pltpu.VMEM(square, f32)],
        pl.CostEstimate(flops=4 * size**3, transcendentals=0, bytes_accessed=160 * size * size),
    )
    (late,) = call(functools.partial(late_total, n_depth), [late], [], [(size // 2, 2 * size)], [])
    other = lax.ppermute(late, "depth", [(i, i ^ 1) for i in range(n_depth)])
    solution, residual = call(
        functools.partial(finish, n_depth),
        [late, other] + list(solved) + mapped + base + image, [], [narrow, narrow], [pltpu.VMEM((3 * size, points), f32)],
    )
    return solution, residual


def solution(mesh):
    return jax.shard_map(
        per_device,
        mesh=mesh,
        in_specs=(
            P("depth", ("row", "col")),
            P("row", "col", None, None, None),
            P("row", "col", None),
            P("row", "col", None),
            P("row", "col"),
        ),
        out_specs=(P("depth", ("row", "col")), P("depth", ("row", "col"))),
        check_vma=False,
    )
```

```python
import functools

import jax
import jax.numpy as jnp
from jax import lax
from jax.experimental import pallas as pl
from jax.experimental.pallas import tpu as pltpu
from jax.sharding import PartitionSpec as P


BLK = 256
SEG = 2
PIVOT = 8
PANEL = 16
HIGHEST = lax.Precision.HIGHEST
VMEM = pl.BlockSpec(memory_space=pltpu.VMEM)
SMEM = pl.BlockSpec(memory_space=pltpu.SMEM)
PARAMS = pltpu.CompilerParams(vmem_limit_bytes=40 << 20)


def partner(index, step, size):
    return index ^ step if size & (size - 1) == 0 else (index + step) % size


def power_of_two(n):
    return n & (n - 1) == 0


def send_all(arrays, axis):
    size = lax.axis_size(axis)
    return [send(arrays[k - 1], axis, k) for k in range(1, size)]


def send(x, axis, step):
    size = lax.axis_size(axis)
    return lax.ppermute(x, axis, [(i, partner(i, step, size)) for i in range(size)])


def collect(x, axis):
    size = lax.axis_size(axis)
    if not power_of_two(size):
        return send_all([x] * (size - 1), axis)
    held = {0: x}
    for k in sorted(range(1, size), key=lambda k: (k.bit_count(), -k)):
        low = k & -k
        held[k] = send(held[k - low], axis, low)
    return [held[k] for k in range(1, size)]


def source_of(axis, step):
    index, size = lax.axis_index(axis), lax.axis_size(axis)
    if size & (size - 1) == 0:
        return index ^ step
    return lax.rem(index + size - step, size)


def partner_of(axis, step):
    index, size = lax.axis_index(axis), lax.axis_size(axis)
    if size & (size - 1) == 0:
        return index ^ step
    return lax.rem(index + step, size)


def dot_nt(a, b):
    return lax.dot_general(a, b, (((1,), (1,)), ((), ())), precision=HIGHEST, preferred_element_type=jnp.float32)


def dot_tn(a, b):
    return lax.dot_general(a, b, (((0,), (0,)), ((), ())), precision=HIGHEST, preferred_element_type=jnp.float32)


def dot_nn(a, b):
    return lax.dot_general(a, b, (((1,), (0,)), ((), ())), precision=HIGHEST, preferred_element_type=jnp.float32)


def halves(x):
    high = x.astype(jnp.bfloat16)
    return high, (x - high.astype(jnp.float32)).astype(jnp.bfloat16)


def bf16_dot(a, b, contract):
    return lax.dot_general(a, b, (contract, ((), ())), preferred_element_type=jnp.float32)


def stack_fields(all_ref, own_ref, depth_refs):
    width, points = own_ref.shape[0], all_ref.shape[1]
    for step, ref in enumerate([own_ref] + depth_refs):
        place = source_of("depth", step)
        all_ref[pl.ds(pl.multiple_of(place * width, width), width), :] = ref[:, 0:points]


def prepare(count_ref, rows_ref, cols_ref, blocks_ref, blocks_out, table_out, rows_at, cols_at, places, sems):
    slots = blocks_ref.shape[2]
    copies = [pltpu.make_async_copy(blocks_ref.at[0, 0, s], blocks_out.at[s], sems.at[s]) for s in range(slots)]
    small = [
        pltpu.make_async_copy(rows_ref, rows_at, sems.at[slots]),
        pltpu.make_async_copy(cols_ref, cols_at, sems.at[slots + 1]),
    ]
    for copy in small + copies:
        copy.start()
    for copy in small:
        copy.wait()
    for slot in range(slots):
        places[0, slot] = rows_at[0, 0, slot]
        places[1, slot] = cols_at[0, 0, slot]
        places[2, slot] = count_ref[0, 0]
    table = pltpu.make_async_copy(places, table_out, sems.at[slots + 2])
    table.start()
    for copy in copies:
        copy.wait()
    table.wait()


def products(
    table_ref, blocks_ref, own_ref, z_refs, y_refs, own_out, z_outs, y_outs,
    col_in, row_in, col_acc, row_acc,
):
    width = own_ref.shape[0]
    row_at, col_at = lax.axis_index("row"), lax.axis_index("col")
    for axis, refs, held in (("row", [own_ref] + z_refs, col_in), ("col", [own_ref] + y_refs, row_in)):
        for step, ref in enumerate(refs):
            place = source_of(axis, step)
            for part in range(SEG):
                high, low = halves(ref[:, part * BLK : (part + 1) * BLK])
                held[place * SEG + part] = jnp.concatenate([high, low], axis=0)
    col_acc[...] = jnp.zeros_like(col_acc)
    row_acc[...] = jnp.zeros_like(row_acc)
    count = table_ref[2, 0]
    for slot in range(blocks_ref.shape[0]):
        high, low = halves(blocks_ref[slot])
        row_place, col_place = table_ref[0, slot], table_ref[1, slot]
        live = slot < count
        for vec, acc, at_in, at_out, contract in (
            (col_in, row_acc, col_place, row_place, ((1,), (1,))),
            (row_in, col_acc, row_place, col_place, ((1,), (0,))),
        ):
            if slot < SEG and acc is col_acc:
                continue
            both = vec[at_in]
            wide = bf16_dot(both, high, contract)
            term = wide[:width] + wide[width:] + bf16_dot(both[:width], low, contract)
            acc[at_out] += jnp.where(live, term, 0.0)
    for part in range(SEG):
        lanes = slice(part * BLK, (part + 1) * BLK)
        own_out[:, lanes] = row_acc[col_at * SEG + part] + col_acc[row_at * SEG + part]
        for step, ref in enumerate(z_outs, 1):
            ref[:, lanes] = col_acc[partner_of("row", step) * SEG + part]
        for step, ref in enumerate(y_outs, 1):
            ref[:, lanes] = row_acc[partner_of("col", step) * SEG + part]


def split(refs, *sizes):
    out = []
    for size in sizes:
        out.append(list(refs[:size]))
        refs = refs[size:]
    return out


def first_products(n_row, n_col, *refs):
    (head, own, z_in, y_in, outs, z_outs, y_outs, scratch) = split(
        refs, 2, 1, n_row - 1, n_col - 1, 2, n_row - 1, n_col - 1, 4
    )
    outs[1][...] = own[0][...]
    products(*head, own[0], z_in, y_in, outs[0], z_outs, y_outs, *scratch)


def first_combine(n_row, n_col, *refs):
    partial, received, out = split(refs, 1, n_row + n_col - 2, 1)
    total = partial[0][...]
    for ref in received:
        total += ref[...]
    out[0][...] = total


def first_grams(n_depth, *refs):
    image, field_refs, out, fields = split(refs, 1, n_depth, 1, 1)
    total = image[0][...]
    points = total.shape[1]
    stack_fields(fields[0], field_refs[0], field_refs[1:])
    everything = fields[0][...]
    out[0][:, :points] = total
    out[0][:, points:] = jnp.concatenate(
        [dot_nt(field_refs[0][...], everything), dot_nt(total, everything)], axis=1
    )


def second_products(n_row, n_col, *refs):
    (head, own, z_in, y_in, outs, z_outs, y_outs, scratch) = split(
        refs, 2, 1, n_row - 1, n_col - 1, 2, n_row - 1, n_col - 1, 4
    )
    points = outs[0].shape[1]
    products(*head, own[0], z_in, y_in, outs[0], z_outs, y_outs, *scratch)
    grams = own[0][:, points:]
    for ref in y_in:
        grams += ref[:, points:]
    outs[1][...] = grams
    for ref in z_outs:
        ref[:, points:] = grams


def second_combine(n_row, n_col, n_depth, *refs):
    partial, gram, z_in, y_in, base_refs, image_refs, out_wide, out_gram, fields = split(
        refs, 1, 1, n_row - 1, n_col - 1, n_depth, n_depth, 1, 1, 1
    )
    points = partial[0].shape[1]
    total = partial[0][...]
    early = gram[0][...]
    for ref in z_in:
        total += ref[:, :points]
        early += ref[:, points:]
    for ref in y_in:
        total += ref[...]
    out_wide[0][:, :points] = total
    out_wide[0][:, points:] = early
    stack_fields(fields[0], base_refs[0], base_refs[1:])
    third = dot_nt(total, fields[0][...])
    stack_fields(fields[0], image_refs[0], image_refs[1:])
    fourth = dot_nt(total, fields[0][...])
    width = total.shape[0]
    packed = [jnp.concatenate([g[: width // 2], g[width // 2 :]], axis=1) for g in (third, fourth)]
    for i in range(out_gram[0].shape[0]):
        out_gram[0][i] = packed[i % n_depth % 2]


def factor_two(e):
    a, b, d = e(0, 0), e(0, 1), e(1, 1)
    scale = 1.0 / (a * d - b * b)
    a, b, d = a * scale, b * scale, d * scale
    return lambda q: [d * q[0] - b * q[1], a * q[1] - b * q[0]]


def factor(e, size):
    if size == 2:
        return factor_two(e)
    half = size // 2
    top = factor(e, half)
    columns = [top([e(i, half + j) for i in range(half)]) for j in range(half)]

    def schur(i, j):
        return e(half + i, half + j) - sum(e(a, half + i) * columns[j][a] for a in range(half))

    entries = {(i, j): schur(i, j) for i in range(half) for j in range(i, half)}
    bottom = factor(lambda i, j: entries[i, j], half)

    def solve(q):
        upper = top(q[:half])
        lower = bottom([q[half + i] - sum(columns[i][a] * q[a] for a in range(half)) for i in range(half)])
        return [upper[a] - sum(columns[i][a] * lower[i] for i in range(half)) for a in range(half)] + lower

    return solve


def eliminate(table, size, pivot, panel):
    rows, wide = table.shape
    sub = 8
    at_row = lax.broadcasted_iota(jnp.int32, (sub, wide), 0)
    one = table[:sub] * 0.0 + 1.0
    for start in range(0, size, panel):
        stop = start + panel
        tiles = [table[t : t + sub] for t in range(start, stop, sub)]
        for k in range(start, stop, pivot):
            home, base = (k - start) // sub, k % sub
            spread = [
                [jnp.broadcast_to(tile[:, k + j : k + j + 1], (sub, wide)) for tile in tiles] for j in range(pivot)
            ]
            row = [jnp.broadcast_to(tiles[home][base + i : base + i + 1], (sub, wide)) for i in range(pivot)]
            near = [spread[j][home] * one for j in range(pivot)]
            entries = {
                (i, j): jnp.broadcast_to(near[j][base + i : base + i + 1], (sub, wide))
                for j in range(pivot)
                for i in range(j + 1)
            }
            solved = factor(lambda i, j: entries[i, j], pivot)(row)
            for t, tile in enumerate(tiles):
                tiles[t] = tile - sum(spread[j][t] * solved[j] for j in range(pivot))
                if t == home:
                    for i in range(pivot):
                        tiles[t] = jnp.where(at_row == base + i, solved[i], tiles[t])
        done = jnp.concatenate(tiles, axis=0)
        others = [table[at:to] for at, to in ((0, start), (stop, rows)) if at < to]
        others = [part - dot_nn(part[:, start:stop], done) for part in others]
        table = jnp.concatenate(others[:1] + [done] + others[1:] if start else [done] + others, axis=0)
    return table


def identity_of(size):
    shape = (size, size)
    same = lax.broadcasted_iota(jnp.int32, shape, 0) == lax.broadcasted_iota(jnp.int32, shape, 1)
    return same.astype(jnp.float32)


def early_solve(n_depth, points, *refs):
    wide_refs, outs, scratch = split(refs, n_depth, 3, 1)
    width = wide_refs[0].shape[0]
    size = n_depth * width
    for step, ref in enumerate(wide_refs):
        place = source_of("depth", step)
        scratch[0][pl.ds(pl.multiple_of(place * width, width), width), :] = ref[:, points + size : points + 2 * size]
    gram1 = scratch[0][...]
    first = eliminate(jnp.concatenate([gram1, identity_of(size)], axis=1), size, PIVOT, size)
    inverse = first[:, size:]
    outs[0][...] = inverse
    outs[1][...] = dot_nt(inverse, wide_refs[0][:, points : points + size])
    outs[2][...] = dot_nt(identity_of(size), wide_refs[0][:, points + size : points + 2 * size])


def late_total(n_depth, gathered_ref, out_ref):
    rows = gathered_ref.shape[1]
    groups = gathered_ref.shape[0] // n_depth
    for d in range(n_depth):
        out_ref[d * rows : (d + 1) * rows, :] = sum(gathered_ref[g * n_depth + d] for g in range(groups))


def unpacked(packed, rows):
    size = packed.shape[1] // 2
    parts = []
    for at in range(0, packed.shape[0], rows):
        part = packed[at : at + rows]
        parts += [part[:, :size], part[:, size:]]
    return jnp.concatenate(parts, axis=0)


def finish(n_depth, *refs):
    late, solved, wide_refs, base_refs, image_refs, outs, scratch = split(
        refs, 2, 3, n_depth, n_depth, n_depth, 2, 1
    )
    (fields,) = scratch
    solution_out, residual_out = outs
    width, _ = solution_out.shape
    size = n_depth * width
    for i, refs_of in enumerate((base_refs, image_refs, wide_refs)):
        stack_fields(fields.at[i * size : (i + 1) * size], refs_of[0], refs_of[1:])
    mine, other = (unpacked(ref[...], width // 2) for ref in late)
    even = lax.axis_index("depth") % 2 == 0
    gram2, gram3 = jnp.where(even, mine, other), jnp.where(even, other, mine)
    inverse, start, gram1_own = (ref[...] for ref in solved)
    carry = dot_nn(inverse, gram2)
    schur = gram3 - dot_nn(gram2, carry)
    right = gram1_own - dot_nn(gram2, start)
    fill = jnp.zeros((size, size - width), jnp.float32)
    rows = [jnp.concatenate(parts, axis=1) for parts in ((schur, right, fill), (carry, start, fill))]
    weights = eliminate(jnp.concatenate(rows, axis=0), size, PIVOT, PANEL)[:, size : size + width]
    weight1, weight0, none = weights[:size], weights[size:], jnp.zeros((size, width), jnp.float32)
    both = [jnp.concatenate(parts, axis=1) for parts in ((weight0, none), (weight1, weight0), (none, weight1))]
    result = dot_tn(jnp.concatenate(both, axis=0), fields[...])
    solution_out[...] = result[:width]
    residual_out[...] = base_refs[0][...] - result[width:]


def call(body, operands, in_specs, out_shapes, scratch, cost=None, out_specs=None):
    return pl.pallas_call(
        body,
        out_shape=[s if hasattr(s, "dtype") else jax.ShapeDtypeStruct(s, jnp.float32) for s in out_shapes],
        in_specs=list(in_specs) + [VMEM] * (len(operands) - len(in_specs)),
        out_specs=out_specs or [VMEM] * len(out_shapes),
        scratch_shapes=scratch,
        compiler_params=PARAMS,
        cost_estimate=cost,
    )(*operands)


def per_device(right_sides, blocks, block_rows, block_cols, block_count):
    n_row, n_col, n_depth = (lax.axis_size(a) for a in ("row", "col", "depth"))
    width, points = right_sides.shape
    size = n_depth * width
    slots = blocks.shape[2]
    f32, b16 = jnp.float32, jnp.bfloat16
    work = [
        pltpu.VMEM((n_row * SEG, 2 * width, BLK), b16),
        pltpu.VMEM((n_col * SEG, 2 * width, BLK), b16),
        pltpu.VMEM((n_row * SEG, width, BLK), f32),
        pltpu.VMEM((n_col * SEG, width, BLK), f32),
    ]
    fields = pltpu.VMEM((size, points), f32)
    narrow, wide, tail, square = (width, points), (width, points + 2 * size), (width, 2 * size), (size, size)

    y = send_all([right_sides] * (n_col - 1), "col")
    z = send_all([right_sides] * (n_row - 1), "row")
    near, table = call(
        prepare,
        [block_count] + [pltpu.with_memory_space_constraint(x, pltpu.HBM) for x in (block_rows, block_cols, blocks)],
        [SMEM] + [pl.BlockSpec(memory_space=pltpu.HBM)] * 3,
        [blocks.shape[2:], jax.ShapeDtypeStruct((3, slots), jnp.int32)],
        [pltpu.SMEM(block_rows.shape, jnp.int32)] * 2
        + [pltpu.SMEM((3, slots), jnp.int32), pltpu.SemaphoreType.DMA((slots + 3,))],
        pl.CostEstimate(flops=0, transcendentals=0, bytes_accessed=8 * blocks.size),
        [VMEM, VMEM],
    )
    head = [table, near]
    partial, copied, *rest = call(
        functools.partial(first_products, n_row, n_col),
        head + [right_sides] + z + y, [SMEM], [narrow] * (n_row + n_col), work,
    )
    y = send_all(rest[n_row - 1 :], "col")
    z = send_all(rest[: n_row - 1], "row")
    base = [right_sides] + collect(copied, "depth")
    (image,) = call(functools.partial(first_combine, n_row, n_col), [partial] + z + y, [], [narrow], [])
    z = send_all([image] * (n_row - 1), "row")
    (image_wide,) = call(functools.partial(first_grams, n_depth), [image] + base, [], [wide], [fields])
    y = send_all([image_wide] * (n_col - 1), "col")
    image = [image] + collect(image, "depth")
    partial, gram, *rest = call(
        functools.partial(second_products, n_row, n_col),
        head + [image_wide] + z + y, [SMEM],
        [narrow, tail] + [wide] * (n_row - 1) + [narrow] * (n_col - 1), work,
    )
    y = send_all(rest[n_row - 1 :], "col")
    z = send_all(rest[: n_row - 1], "row")
    n_all = n_row * n_col * n_depth
    mapped, late = call(
        functools.partial(second_combine, n_row, n_col, n_depth),
        [partial, gram] + z + y + base + image, [], [wide, (n_all, width // 2, 2 * size)], [fields],
    )
    mapped = [mapped] + collect(mapped, "depth")
    late = lax.all_to_all(late, ("row", "col", "depth"), 0, 0)
    solved = call(
        functools.partial(early_solve, n_depth, points), mapped, [],
        [square, (size, width), (size, width)], [pltpu.VMEM(square, f32)],
        pl.CostEstimate(flops=4 * size**3, transcendentals=0, bytes_accessed=160 * size * size),
    )
    (late,) = call(functools.partial(late_total, n_depth), [late], [], [(size // 2, 2 * size)], [])
    other = lax.ppermute(late, "depth", [(i, i ^ 1) for i in range(n_depth)])
    solution, residual = call(
        functools.partial(finish, n_depth),
        [late, other] + list(solved) + mapped + base + image, [], [narrow, narrow], [pltpu.VMEM((3 * size, points), f32)],
    )
    return solution, residual


def solution(mesh):
    return jax.shard_map(
        per_device,
        mesh=mesh,
        in_specs=(
            P("depth", ("row", "col")),
            P("row", "col", None, None, None),
            P("row", "col", None),
            P("row", "col", None),
            P("row", "col"),
        ),
        out_specs=(P("depth", ("row", "col")), P("depth", ("row", "col"))),
        check_vma=False,
    )
```
